128 devices in a mesh: row: 8 (over y_lo, x), col: 16 (over y_hi, z, core).
Axes of the slice: x: 4, y: 4 (y_hi: 2, y_lo: 2; y = y_hi * 2 + y_lo), z: 4, core: 2. Of those that a mesh axis runs over, the one named last changes fastest.
Arguments:
- sign_iterate: bfloat16 [8192, 8192], P('row', 'col'), may hold values from -6 to 6
- sign_square: bfloat16 [8192, 8192], P('row', 'col'), may hold values from -0.125 to 0.125
- pattern_x: int32 [64, 64], P('row', 'col'), may hold values 0 or 1
- pattern_y: int32 [64, 64], P('row', 'col'), may hold values 0 or 1
- pattern_product: int32 [64, 64], P('row', 'col'), may hold values 0 or 1
- orbital_energy: bfloat16 [8192], P('row'), may hold values from -3 to 1
- pair_dest: int32 [128, 128, 1], P(('row', 'col')), may hold values from 0 to 127; in each aligned block of 128 rows (0 to 127, 128 to 255, ..., all dimensions but the last counted through in order) at most 2 rows name the same one
- pair_block: int32 [128, 128], P(('row', 'col')), may hold values from 0 to 31
- force_h: bfloat16 [32768, 128, 128], P(('row', 'col')), may hold values from -0.5 to 0.5
- force_s: bfloat16 [32768, 128, 128], P(('row', 'col')), may hold values from -0.5 to 0.5
Outputs:
- sign_next: bfloat16 [8192, 8192], P('row', 'col')
- forces: float32 [32768], P(('row', 'col'))
The draws below stay inside these ranges and needn't reach their ends.
Inputs may be any that keep to these rules, and one draw needn't show every extreme that they name: `pair_dest`: among the 128 entries of one device no owner is named more than 2 times, a bound that some block reaches. `pair_block`: A row-major index into the device's own 8 x 4 grid of blocks.
All inputs are finite; a program needn't handle non-finite values. No bound on the sum of `pattern_x` or of `pattern_y` or of `pattern_product` on one device may be relied on, other than what follows from the above.
Results may differ from the reference program's by a relative error of at most 0.003.
Values may be sent and summed in bfloat16 or wider, within the bound.
No kernel may reach another device: no remote copies, remote signals or barrier semaphores. Data moves between devices by JAX's collectives and lax.ppermute only.
A program may use at most 128 MiB of HBM per device.

```python
import math
import jax
import jax.numpy as jnp
import numpy as np
from jax import lax

BS = 128
QB = 4
CAP = 2
NBT = 64
ORDER = 8192
MB_DEV = 8
BLK_DEV = 32
PAIRS_DEV = 128
N_ROW = 8
N_COL = 16


def touch_ends(result, key, least, largest):
    place = [jax.random.randint(jax.random.fold_in(key, axis), (), 0, length) for axis, length in enumerate(result.shape)]
    longest = result.shape.index(max(result.shape))
    neighbour = place[:longest] + [(place[longest] + 1) % result.shape[longest]] + place[longest + 1:]
    return result.at[tuple(place)].set(least).at[tuple(neighbour)].set(largest)


def levels(stream_key, shape, pieces, low, top_value):
    level, own = 1.0, jax.random.fold_in(stream_key, 6)
    for position, parts in pieces:
        draws = jnp.exp(jax.random.uniform(jax.random.fold_in(own, position), (parts,), jnp.float32, low / len(pieces), top_value / len(pieces)))
        level = level * jnp.repeat(draws, shape[position] // parts).reshape([-1 if axis == position else 1 for axis in range(len(shape))])
    return level


def assign_block(rng, own, number, rows, amount, top, bound, skew):
    ranking = jax.random.permutation(rng, amount)
    heavy_load, ordinary = load_shares(amount, rows * top, bound, skew, True), load_shares(amount, rows * top, bound, skew, False)
    places = jnp.arange(amount)

    def named(tallies, offset_by):
        used = int((tallies > 0).sum())
        fixed = max(1, used // 4)
        moved = fixed + (places - fixed + offset_by * (used - fixed)) % max(1, amount - fixed)
        return jnp.zeros((amount,), jnp.int32).at[ranking[jnp.where(places < fixed, places, moved)]].set(jnp.asarray(tallies, jnp.int32))

    tallies = jnp.where(number % 4 == 0, named(heavy_load, number // 4), named(ordinary, number - number // 4 - 1))
    mixed = jax.random.permutation(jax.random.fold_in(own, 3), amount)
    donor, taker = mixed[0:amount // 2 * 2:2], mixed[1:amount // 2 * 2:2]
    room = jnp.minimum(tallies[donor] - 1, bound - tallies[taker]) // 2
    room = jnp.where((donor == ranking[0]) | (taker == ranking[0]) | (tallies[taker] == 0), 0, jnp.maximum(room, 0))
    moved = jax.random.randint(jax.random.fold_in(own, 4), (amount // 2,), 0, 1 << 20) % (room + 1)
    tallies = tallies.at[donor].add(-moved).at[taker].add(moved)
    members = jnp.searchsorted(jnp.cumsum(tallies), jnp.arange(rows * top), side="right").astype(jnp.int32)
    table = members.reshape(top, rows).T
    table = table[jax.random.permutation(jax.random.fold_in(own, 1), rows)]
    offset_by = jax.random.randint(jax.random.fold_in(own, 2), (rows, 1), 0, top)
    return jnp.take_along_axis(table, (jnp.arange(top)[None, :] + offset_by) % top, axis=1)


def load_shares(number_of, total, limit, lean, full):
    loads = [(1 << 20) // math.isqrt(standing ** lean) + 1 for standing in range(1, number_of + 1)]
    largest = limit if full else min(limit, max(-(-total // number_of), total * loads[0] // sum(loads)))
    least = 1 if total - largest >= number_of - 1 else 0
    holding, surplus = [largest] + [least] * (number_of - 1), total - largest - least * (number_of - 1)
    while surplus > 0:
        movable = [i for i in range(1, number_of) if holding[i] < largest] or [i for i in range(1, number_of) if holding[i] < limit]
        whole, budget = sum([loads[i] for i in movable]), surplus
        for i in movable:
            addition = min(limit - holding[i], max(1, budget * loads[i] // whole), surplus)
            holding[i] = holding[i] + addition
            surplus = surplus - addition
    return np.array(holding)


def bell_draw(rng, dims, width, most, split=(), held_as=jnp.bfloat16):
    level = levels(rng, dims, split, -0.22, 0.18) if split else 1.0
    array = jax.random.normal(rng, dims, jnp.float32) * width * level
    return jnp.minimum(jnp.maximum(array, -most), most).astype(held_as)


def setup_inputs(seed: int = 0) -> dict:
    splits = jax.random.split(jax.random.key(seed), 11)
    sign_iterate = bell_draw(splits[0], (ORDER, ORDER), 1.0, 6.0, ((0, 8), (1, 16)))
    sign_square = bell_draw(splits[1], (ORDER, ORDER), (ORDER // 4) ** -0.5, 0.125, ((0, 8), (1, 16)))
    pattern_x = touch_ends((jax.random.randint(splits[2], (NBT, NBT), 0, 2) < 1).astype(jnp.int32), jax.random.fold_in(splits[2], 1), 0, 1)
    pattern_y = touch_ends((jax.random.randint(splits[3], (NBT, NBT), 0, 2) < 1).astype(jnp.int32), jax.random.fold_in(splits[3], 1), 0, 1)
    pattern_product = touch_ends((jax.random.randint(splits[4], (NBT, NBT), 0, 4) < 3).astype(jnp.int32), jax.random.fold_in(splits[4], 1), 0, 1)
    orbital_energy = jnp.clip(-3.0 + 4.0 * jax.random.uniform(splits[5], (ORDER,), jnp.float32) ** levels(splits[5], (ORDER,), ((0, 8),), -0.2, 0.2), -3.0, 1.0).astype(jnp.bfloat16)
    pair_dest_keys = jax.random.split(jax.random.fold_in(splits[6], 1), (N_ROW * N_COL) * PAIRS_DEV // PAIRS_DEV)
    pair_dest_turns = jax.random.permutation(jax.random.fold_in(splits[6], 3), (N_ROW * N_COL) * PAIRS_DEV // PAIRS_DEV)
    pair_dest = jax.vmap(lambda own, number: assign_block(jax.random.fold_in(splits[6], 2), own, number, PAIRS_DEV, N_ROW * N_COL, 1, CAP, 2))(pair_dest_keys, pair_dest_turns).reshape((N_ROW * N_COL, PAIRS_DEV, 1))
    pair_block = touch_ends(jax.random.randint(splits[7], (N_ROW * N_COL, PAIRS_DEV), 0, BLK_DEV), jax.random.fold_in(splits[7], 1), 0, BLK_DEV - 1).astype(jnp.int32)
    force_h = bell_draw(splits[8], (N_ROW * N_COL * N_ROW * N_COL * CAP, BS, BS), BS ** -0.5, 0.5, ((0, 128),))
    force_s = bell_draw(splits[9], (N_ROW * N_COL * N_ROW * N_COL * CAP, BS, BS), BS ** -0.5, 0.5, ((0, 128),))
    return {"sign_iterate": sign_iterate, "sign_square": sign_square, "pattern_x": pattern_x, "pattern_y": pattern_y, "pattern_product": pattern_product, "orbital_energy": orbital_energy, "pair_dest": pair_dest, "pair_block": pair_block, "force_h": force_h, "force_s": force_s}


def apply_pattern(matrix, pattern):
    blocks = matrix.reshape(NBT, BS, NBT, BS) * pattern[:, None, :, None].astype(matrix.dtype)
    return blocks.reshape(ORDER, ORDER)


def reference(sign_iterate, sign_square, pattern_x, pattern_y, pattern_product, orbital_energy, pair_dest, pair_block, force_h, force_s):
    xmask = apply_pattern(sign_iterate, pattern_x)
    ymask = apply_pattern(sign_square, pattern_y)
    product = jnp.dot(xmask, ymask, preferred_element_type=jnp.float32)
    product = apply_pattern(product, pattern_product)
    xnew = 1.5 * xmask.astype(jnp.float32) - 0.5 * product
    sign_next = xnew.astype(jnp.bfloat16)
    diag_index = jnp.arange(ORDER)
    half_dens = (-0.5 * xnew).at[diag_index, diag_index].add(0.5)
    density = half_dens.astype(jnp.bfloat16)
    energy_f = orbital_energy.astype(jnp.float32)
    devices = N_ROW * N_COL
    dest = pair_dest[:, :, 0]
    same = dest[:, :, None] == dest[:, None, :]
    earlier = jnp.arange(PAIRS_DEV)[None, :] < jnp.arange(PAIRS_DEV)[:, None]
    rank = jnp.sum((same & earlier[None, :, :]).astype(jnp.int32), axis=2)
    dev_ids = jnp.arange(devices, dtype=jnp.int32)[:, None]
    block_row = (dev_ids // N_COL) * MB_DEV + pair_block // QB
    block_col = (dev_ids % N_COL) * QB + pair_block % QB
    slot = dest * (devices * CAP) + dev_ids * CAP + rank

    def one_pair(item):
        brow, bcol, where = item
        dblk = lax.dynamic_slice(density, (brow * BS, bcol * BS), (BS, BS)).astype(jnp.float32)
        eblk = lax.dynamic_slice_in_dim(energy_f, brow * BS, BS, 0)
        hblk = lax.dynamic_index_in_dim(force_h, where, 0, keepdims=False).astype(jnp.float32)
        sblk = lax.dynamic_index_in_dim(force_s, where, 0, keepdims=False).astype(jnp.float32)
        return jnp.sum(dblk * hblk) - jnp.sum(eblk[:, None] * dblk * sblk)

    values = lax.map(one_pair, (block_row.reshape(-1).astype(jnp.int32), block_col.reshape(-1).astype(jnp.int32), slot.reshape(-1).astype(jnp.int32)))
    forces = jnp.zeros((devices * devices * CAP,), jnp.float32).at[slot.reshape(-1)].set(values)
    return sign_next, forces
```

```python
import jax
import jax.numpy as jnp
from jax import lax
from jax.experimental import pallas as pl
from jax.experimental.pallas import tpu as pltpu
from jax.sharding import Mesh, PartitionSpec as P

BS = 128
QB = 4
CAP = 2
RB = 8
BLOCKS = RB * QB
ROWS = RB * BS
COLS = QB * BS
RING = 4
AXES = ("yl", "x", "yh", "z", "c")
SWAP = [(0, 1), (1, 0)]
UP = [(i, (i + 1) % RING) for i in range(RING)]
DOWN = [(i, (i - 1) % RING) for i in range(RING)]


def mask_kernel(px_ref, py_ref, x_ref, y_ref, xo_ref, yo_ref):
    i = pl.program_id(0)
    for r in range(2):
        for j in range(QB):
            rows, cols = slice(r * BS, (r + 1) * BS), slice(j * BS, (j + 1) * BS)
            for p_ref, in_ref, out_ref in ((px_ref, x_ref, xo_ref), (py_ref, y_ref, yo_ref)):
                keep = (p_ref[i * 2 + r, j] > 0).astype(jnp.float32).astype(jnp.bfloat16)
                out_ref[rows, cols] = in_ref[rows, cols] * keep


def masked_tiles(x, y, pattern_x, pattern_y):
    tile = pl.BlockSpec((2 * BS, COLS), lambda i: (i, 0))
    smem = pl.BlockSpec(memory_space=pltpu.SMEM)
    return pl.pallas_call(
        mask_kernel,
        grid=(RB // 2,),
        in_specs=[smem, smem, tile, tile],
        out_specs=[tile, tile],
        out_shape=[jax.ShapeDtypeStruct((ROWS, COLS), jnp.bfloat16)] * 2,
        cost_estimate=pl.CostEstimate(flops=2 * ROWS * COLS, bytes_accessed=8 * ROWS * COLS, transcendentals=0),
        name="mask_tiles",
    )(pattern_x, pattern_y, x, y)


def ring_gather(tile, axis):
    half = ROWS // 2
    below = lax.ppermute(tile, axis, UP)
    above = lax.ppermute(tile, axis, DOWN)
    far_top = lax.ppermute(below[:half], axis, UP)
    far_bottom = lax.ppermute(above[half:], axis, DOWN)
    return [tile, below, above, far_top, far_bottom]


def product_kernel(*refs):
    x_own, x_peer, y_in = refs[:10], refs[10:20], refs[20:30]
    where_ref, pattern_ref, index_ref, xm_ref = refs[30:34]
    sign_ref, payload_ref = refs[34:36]
    x_buf, y_buf, acc, dens, x_sem, y_sem, out_sem = refs[36:]
    yl, xi, yh, z, core = (where_ref[k] for k in range(5))
    half = ROWS // 2
    own_cols = pl.ds(pl.multiple_of(core * COLS, COLS), COLS)
    peer_cols = pl.ds(pl.multiple_of((1 - core) * COLS, COLS), COLS)

    def place(group, member):
        position = group * 4 + min(member, 3)
        rows = {3: pl.ds(0, half), 4: pl.ds(half, half)}.get(member, pl.ds(0, ROWS))
        return position, rows

    for group in range(2):
        for member in range(5):
            position, rows = place(group, member)
            pltpu.make_async_copy(
                y_in[group * 5 + member], y_buf.at[position, rows], y_sem.at[position]
            ).start()
    for group in range(2):
        for member in range(5):
            position, rows = place(group, member)
            for source, cols in ((x_own, own_cols), (x_peer, peer_cols)):
                pltpu.make_async_copy(
                    source[group * 5 + member], x_buf.at[position, rows, cols], x_sem.at[position]
                ).start()

    acc[...] = jnp.zeros_like(acc)
    for position in range(8):
        pltpu.make_async_copy(y_buf.at[position], y_buf.at[position], y_sem.at[position]).wait()

    def step(position, carry):
        pltpu.make_async_copy(x_buf.at[position], x_buf.at[position], x_sem.at[position]).wait()
        group, member = position // 4, position % 4
        offset = jnp.where(member == 0, 0, jnp.where(member == 1, 3, jnp.where(member == 2, 1, 2)))
        t = yh ^ group
        s = (z + offset) % RING
        gap = (s - xi + RING) % RING
        y_member = jnp.where(gap == 0, 0, jnp.where(gap == 3, 1, jnp.where(gap == 1, 2, 3)))
        y_position = (t ^ yl) * 4 + y_member
        for part in range(2):
            rows = slice(part * half, (part + 1) * half)
            acc[rows, :] += jnp.dot(
                x_buf[position, rows, :], y_buf[y_position], preferred_element_type=jnp.float32
            )
        return carry

    lax.fori_loop(0, 8, step, 0)

    block_row = (yl * 4 + xi) * RB
    block_col = ((yh * 4 + z) * 2 + core) * QB
    same = lax.broadcasted_iota(jnp.int32, (BS, BS), 0) == lax.broadcasted_iota(jnp.int32, (BS, BS), 1)
    half_eye = jnp.where(same, 0.5, 0.0).astype(jnp.float32)

    def finish(i, carry):
        rows = pl.ds(pl.multiple_of(i * BS, BS), BS)
        for j in range(QB):
            cols = slice(j * BS, (j + 1) * BS)
            kept = jnp.where(pattern_ref[i, j] > 0, 0.5, 0.0)
            xnew = 1.5 * xm_ref[rows, cols].astype(jnp.float32) - kept * acc[rows, cols]
            sign_ref[rows, cols] = xnew.astype(jnp.bfloat16)
            on_diagonal = jnp.where(block_row + i == block_col + j, 1.0, 0.0)
            dens[i * QB + j] = (on_diagonal * half_eye - 0.5 * xnew).astype(jnp.bfloat16)
        return carry

    lax.fori_loop(0, RB, finish, 0)
    dens[BLOCKS] = jnp.zeros((BS, BS), jnp.bfloat16)

    slots = payload_ref.shape[0]

    def send(slot, carry):
        pltpu.make_async_copy(dens.at[index_ref[slot]], payload_ref.at[slot], out_sem).start()
        return carry

    lax.fori_loop(0, slots, send, 0)
    pltpu.make_async_copy(payload_ref, payload_ref, out_sem).wait()


def product_and_payload(x_own, x_peer, y_parts, where, pattern, index, xm):
    slots = index.shape[0]
    hbm = pl.BlockSpec(memory_space=pl.ANY)
    smem = pl.BlockSpec(memory_space=pltpu.SMEM)
    vmem = pl.BlockSpec(memory_space=pltpu.VMEM)
    return pl.pallas_call(
        product_kernel,
        in_specs=[hbm] * 30 + [smem] * 3 + [vmem],
        out_specs=[vmem, hbm],
        out_shape=[
            jax.ShapeDtypeStruct((ROWS, COLS), jnp.bfloat16),
            jax.ShapeDtypeStruct((slots, BS, BS), jnp.bfloat16),
        ],
        scratch_shapes=[
            pltpu.VMEM((8, ROWS, 2 * COLS), jnp.bfloat16),
            pltpu.VMEM((8, ROWS, COLS), jnp.bfloat16),
            pltpu.VMEM((ROWS, COLS), jnp.float32),
            pltpu.VMEM((BLOCKS + 1, BS, BS), jnp.bfloat16),
            pltpu.SemaphoreType.DMA((8,)),
            pltpu.SemaphoreType.DMA((8,)),
            pltpu.SemaphoreType.DMA,
        ],
        compiler_params=pltpu.CompilerParams(vmem_limit_bytes=48 * 2**20),
        cost_estimate=pl.CostEstimate(
            flops=2 * ROWS * COLS * 8 * ROWS, bytes_accessed=34 * 2**20, transcendentals=0
        ),
        name="product_payload",
    )(*x_own, *x_peer, *y_parts, where, pattern, index, xm)


FCH = 16


def force_kernel(d_ref, h_ref, s_ref, e_ref, out_ref):
    same = lax.broadcasted_iota(jnp.int32, (BS, BS), 0) == lax.broadcasted_iota(jnp.int32, (BS, BS), 1)
    ones = jnp.ones((BS, BS), jnp.bfloat16)
    for k in range(FCH):
        spread = jnp.where(same, e_ref[k : k + 1, :].astype(jnp.float32), 0.0).astype(jnp.bfloat16)
        energy = jnp.dot(spread, ones, preferred_element_type=jnp.float32)
        term = d_ref[k].astype(jnp.float32) * (
            h_ref[k].astype(jnp.float32) - energy * s_ref[k].astype(jnp.float32)
        )
        out_ref[k : k + 1, :] = jnp.sum(term, axis=0, keepdims=True)


def force_sums(dens, force_h, force_s, energy):
    slots = dens.shape[0]
    block = pl.BlockSpec((FCH, BS, BS), lambda i: (i, 0, 0))
    line = pl.BlockSpec((FCH, BS), lambda i: (i, 0))
    partial = pl.pallas_call(
        force_kernel,
        grid=(slots // FCH,),
        in_specs=[block, block, block, line],
        out_specs=line,
        out_shape=jax.ShapeDtypeStruct((slots, BS), jnp.float32),
        cost_estimate=pl.CostEstimate(
            flops=6 * slots * BS * BS, bytes_accessed=6 * slots * BS * BS, transcendentals=0
        ),
        name="force_sums",
    )(dens, force_h, force_s, energy)
    return jnp.sum(partial, axis=1)


def exchange(payload):
    return lax.all_to_all(payload, AXES, split_axis=0, concat_axis=0, tiled=True)


def shards(x, y, pattern_x, pattern_y, pattern_product, orbital_energy, pair_dest, pair_block, force_h, force_s):
    dest, wanted = pair_dest[0, :, 0], pair_block[0]
    slots = force_h.shape[0]
    entries = dest.shape[0]
    order = jnp.arange(entries, dtype=jnp.int32)
    earlier = (dest[:, None] == dest[None, :]) & (order[None, :] < order[:, None])
    rank = jnp.sum(earlier.astype(jnp.int32), axis=1)
    slot = dest * CAP + rank
    named = slot[None, :] == jnp.arange(slots, dtype=jnp.int32)[:, None]
    index = jnp.sum(jnp.where(named, wanted[None, :] - BLOCKS, 0), axis=1) + BLOCKS
    pick_row = (index[:, None] // QB == jnp.arange(RB, dtype=jnp.int32)[None, :]).astype(jnp.bfloat16)
    send_energy = jnp.dot(
        pick_row, orbital_energy.reshape(RB, BS), preferred_element_type=jnp.float32
    ).astype(jnp.bfloat16)

    xm, ym = masked_tiles(x, y, pattern_x, pattern_y)
    y_far = lax.ppermute(ym, "yl", SWAP)
    x_far = lax.ppermute(xm, "yh", SWAP)
    y_parts = ring_gather(ym, "x") + ring_gather(y_far, "x")
    x_own = ring_gather(xm, "z") + ring_gather(x_far, "z")
    x_peer = [lax.ppermute(part, "c", SWAP) for part in x_own]
    energy = exchange(send_energy)

    where = jnp.stack([lax.axis_index(axis) for axis in AXES]).astype(jnp.int32)
    sign_next, payload = product_and_payload(x_own, x_peer, y_parts, where, pattern_product, index, xm)
    received = exchange(payload)
    return sign_next, force_sums(received, force_h, force_s, energy)


def solution(mesh):
    fine = Mesh(mesh.devices.reshape(2, 4, 2, 4, 2), AXES)
    row, col = ("yl", "x"), ("yh", "z", "c")
    in_specs = (
        P(row, col),
        P(row, col),
        P(row, col),
        P(row, col),
        P(row, col),
        P(row),
        P(AXES, None, None),
        P(AXES, None),
        P(AXES, None, None),
        P(AXES, None, None),
    )
    out_specs = (P(row, col), P(AXES))
    return jax.shard_map(shards, mesh=fine, in_specs=in_specs, out_specs=out_specs, check_vma=False)
```

```python
import jax
import jax.numpy as jnp
from jax import lax
from jax.experimental import pallas as pl
from jax.experimental.pallas import tpu as pltpu
from jax.sharding import Mesh, PartitionSpec as P

BS = 128
QB = 4
CAP = 2
RB = 8
BLOCKS = RB * QB
ROWS = RB * BS
COLS = QB * BS
RING = 4
AXES = ("yl", "x", "yh", "z", "c")
SWAP = [(0, 1), (1, 0)]
UP = [(i, (i + 1) % RING) for i in range(RING)]
DOWN = [(i, (i - 1) % RING) for i in range(RING)]


def mask_x_kernel(p_ref, x_ref, o_ref):
    i = pl.program_id(0)
    for r in range(2):
        for j in range(QB):
            rows, cols = slice(r * BS, (r + 1) * BS), slice(j * BS, (j + 1) * BS)
            keep = (p_ref[j, i * 2 + r] > 0).astype(jnp.float32).astype(jnp.bfloat16)
            o_ref[rows, cols] = x_ref[rows, cols] * keep


def mask_y_kernel(where_ref, p_ref, q_ref, y_ref, z_ref, o_ref):
    first = where_ref[4] * (RB // 2) + pl.program_id(0) * 2
    for r in range(2):
        for j in range(QB):
            rows, cols = slice(r * BS, (r + 1) * BS), slice(j * BS, (j + 1) * BS)
            far_cols = slice(COLS + j * BS, COLS + (j + 1) * BS)
            keep = (p_ref[j, first + r] > 0).astype(jnp.float32).astype(jnp.bfloat16)
            o_ref[rows, cols] = y_ref[rows, cols] * keep
            keep = (q_ref[j, first + r] > 0).astype(jnp.float32).astype(jnp.bfloat16)
            o_ref[rows, far_cols] = z_ref[rows, cols] * keep


SMEM = pl.BlockSpec(memory_space=pltpu.SMEM)
VMEM = pl.BlockSpec(memory_space=pltpu.VMEM)
HBM = pl.BlockSpec(memory_space=pltpu.HBM)


def mask_x(x, pattern):
    tile = pl.BlockSpec((2 * BS, COLS), lambda i: (i, 0))
    return pl.pallas_call(
        mask_x_kernel,
        grid=(RB // 2,),
        in_specs=[SMEM, tile],
        out_specs=tile,
        out_shape=jax.ShapeDtypeStruct((ROWS, COLS), jnp.bfloat16),
        cost_estimate=pl.CostEstimate(flops=ROWS * COLS, bytes_accessed=4 * ROWS * COLS, transcendentals=0),
        name="mask_x",
    )(pattern, x)


def mask_y(y, y_peer, pattern, pattern_peer, where):
    tile = pl.BlockSpec((2 * BS, COLS), lambda i, w: (w[4] * (RB // 4) + i, 0))
    return pl.pallas_call(
        mask_y_kernel,
        grid_spec=pltpu.PrefetchScalarGridSpec(
            num_scalar_prefetch=1,
            grid=(RB // 4,),
            in_specs=[SMEM, SMEM, tile, tile],
            out_specs=pl.BlockSpec((2 * BS, 2 * COLS), lambda i, w: (i, 0)),
        ),
        out_shape=jax.ShapeDtypeStruct((ROWS // 2, 2 * COLS), jnp.bfloat16),
        cost_estimate=pl.CostEstimate(flops=ROWS * COLS, bytes_accessed=4 * ROWS * COLS, transcendentals=0),
        name="mask_y",
    )(where, pattern, pattern_peer, y, y_peer)


def after(value, *others):
    return lax.optimization_barrier((value,) + others)[0]


def y_place(where_ref, position):
    yl, xi, yh, z = (where_ref[k] for k in range(4))
    member = position % 4
    offset = jnp.where(member == 0, 0, jnp.where(member == 1, 3, jnp.where(member == 2, 1, 2)))
    gap = (z + offset - xi + 2 * RING) % RING
    y_member = jnp.where(gap == 0, 0, jnp.where(gap == 3, 1, jnp.where(gap == 1, 2, 3)))
    return (yh ^ (position // 4) ^ yl) * 4 + y_member


X_PIECES = ((0, 0, 2), (1, 0, 2), (2, 0, 2), (3, 0, 1), (3, 1, 1), (4, 0, 1), (4, 1, 1), (5, 0, 1), (5, 1, 1), (6, 0, 1), (6, 1, 1))
Y_PIECES = ((0, 0, 2), (1, 0, 2), (2, 0, 2), (3, 0, 1), (3, 1, 1), (4, 0, 2), (5, 0, 2), (6, 0, 2))
EARLY = 7


def early_kernel(*refs):
    nx, ny = len(X_PIECES), len(Y_PIECES)
    x_in, y_in, where_ref = refs[:nx], refs[nx : nx + ny], refs[nx + ny]
    own_ref, far_ref, x_late, y_late = refs[nx + ny + 1 : nx + ny + 5]
    x_buf, y_buf, x_sem, y_sem = refs[nx + ny + 5 :]

    for k in range(max(nx, ny)):
        for pieces, source, buf, sem, half in (
            (X_PIECES, x_in, x_buf, x_sem, ROWS // 2),
            (Y_PIECES, y_in, y_buf, y_sem, ROWS // 4),
        ):
            if k < len(pieces):
                position, start, size = pieces[k]
                target = buf.at[position, pl.ds(start * half, size * half)]
                pltpu.make_async_copy(source[k], target, sem.at[position]).start()

    own_ref[...] = jnp.zeros_like(own_ref)
    far_ref[...] = jnp.zeros_like(far_ref)

    def step(position, carry):
        pltpu.make_async_copy(x_buf.at[position], x_buf.at[position], x_sem.at[position]).wait()
        y_position = y_place(where_ref, position)

        @pl.when(y_position != EARLY)
        def _():
            pltpu.make_async_copy(y_buf.at[y_position], y_buf.at[y_position], y_sem.at[y_position]).wait()
            for out_ref, cols in ((own_ref, slice(0, COLS)), (far_ref, slice(COLS, 2 * COLS))):
                out_ref[...] += jnp.dot(
                    x_buf[position], y_buf[y_position, :, cols], preferred_element_type=jnp.float32
                )

        @pl.when(y_position == EARLY)
        def _():
            x_late[...] = x_buf[position]

        return carry

    lax.fori_loop(0, EARLY, step, 0)
    last = y_place(where_ref, EARLY)

    @pl.when(last != EARLY)
    def _():
        pltpu.make_async_copy(y_buf.at[last], y_buf.at[last], y_sem.at[last]).wait()
        y_late[...] = y_buf[last]


def early_product(x_parts, y_parts, where):
    return pl.pallas_call(
        early_kernel,
        in_specs=[HBM] * (len(X_PIECES) + len(Y_PIECES)) + [SMEM],
        out_specs=[VMEM] * 4,
        out_shape=[
            jax.ShapeDtypeStruct((ROWS, COLS), jnp.float32),
            jax.ShapeDtypeStruct((ROWS, COLS), jnp.float32),
            jax.ShapeDtypeStruct((ROWS, COLS), jnp.bfloat16),
            jax.ShapeDtypeStruct((ROWS // 2, 2 * COLS), jnp.bfloat16),
        ],
        scratch_shapes=[
            pltpu.VMEM((EARLY, ROWS, COLS), jnp.bfloat16),
            pltpu.VMEM((EARLY, ROWS // 2, 2 * COLS), jnp.bfloat16),
            pltpu.SemaphoreType.DMA((EARLY,)),
            pltpu.SemaphoreType.DMA((EARLY,)),
        ],
        compiler_params=pltpu.CompilerParams(vmem_limit_bytes=36 * 2**20),
        cost_estimate=pl.CostEstimate(
            flops=14 * ROWS * COLS * ROWS, bytes_accessed=20 * 2**20, transcendentals=0
        ),
        name="early_product",
    )(*x_parts, *y_parts, where)


def late_kernel(where_ref, x_top, x_bottom, y_top, y_bottom, x_late, y_late, own_ref, far_ref, own_out, far_out):
    last = y_place(where_ref, EARLY)
    half, quarter = ROWS // 2, ROWS // 4

    def add(same_chunk):
        for sum_ref, out_ref, cols in (
            (own_ref, own_out, slice(0, COLS)),
            (far_ref, far_out, slice(COLS, 2 * COLS)),
        ):
            for rows, x_ref in ((slice(0, half), x_top), (slice(half, ROWS), x_bottom)):
                total = sum_ref[rows, :]
                x_last = x_ref if same_chunk else x_late.at[rows]
                total += jnp.dot(x_last[:, :quarter], y_top[:, cols], preferred_element_type=jnp.float32)
                total += jnp.dot(x_last[:, quarter:], y_bottom[:, cols], preferred_element_type=jnp.float32)
                if not same_chunk:
                    total += jnp.dot(x_ref[...], y_late[:, cols], preferred_element_type=jnp.float32)
                out_ref[rows, :] = total

    pl.when(last == EARLY)(lambda: add(True))
    pl.when(last != EARLY)(lambda: add(False))


def late_product(where, x_far, y_far, x_late, y_late, own, far):
    return pl.pallas_call(
        late_kernel,
        in_specs=[SMEM] + [VMEM] * 8,
        out_specs=[VMEM] * 2,
        out_shape=[jax.ShapeDtypeStruct((ROWS, COLS), jnp.float32)] * 2,
        compiler_params=pltpu.CompilerParams(vmem_limit_bytes=24 * 2**20),
        cost_estimate=pl.CostEstimate(
            flops=4 * ROWS * COLS * ROWS, bytes_accessed=12 * 2**20, transcendentals=0
        ),
        name="late_product",
    )(where, *x_far, *y_far, x_late, y_late, own, far)


def finish_kernel(where_ref, pattern_ref, index_ref, xm_ref, own_ref, peer_ref, sign_ref, payload_ref, dens, out_sem):
    yl, xi, yh, z, core = (where_ref[k] for k in range(5))
    block_row = (yl * 4 + xi) * RB
    block_col = ((yh * 4 + z) * 2 + core) * QB
    same = lax.broadcasted_iota(jnp.int32, (BS, BS), 0) == lax.broadcasted_iota(jnp.int32, (BS, BS), 1)
    half_eye = jnp.where(same, 0.5, 0.0).astype(jnp.float32)

    def finish(i, carry):
        rows = pl.ds(pl.multiple_of(i * BS, BS), BS)
        for j in range(QB):
            cols = slice(j * BS, (j + 1) * BS)
            kept = jnp.where(pattern_ref[j, i] > 0, 0.5, 0.0)
            product = own_ref[rows, cols] + peer_ref[rows, cols]
            xnew = 1.5 * xm_ref[rows, cols].astype(jnp.float32) - kept * product
            sign_ref[rows, cols] = xnew.astype(jnp.bfloat16)
            on_diagonal = jnp.where(block_row + i == block_col + j, 1.0, 0.0)
            dens[i * QB + j] = (on_diagonal * half_eye - 0.5 * xnew).astype(jnp.bfloat16)
        return carry

    lax.fori_loop(0, RB, finish, 0)
    dens[BLOCKS] = jnp.zeros((BS, BS), jnp.bfloat16)

    def send(slot, carry):
        pltpu.make_async_copy(dens.at[index_ref[slot]], payload_ref.at[slot], out_sem).start()
        return carry

    lax.fori_loop(0, payload_ref.shape[0], send, 0)
    pltpu.make_async_copy(payload_ref, payload_ref, out_sem).wait()


def finish_and_payload(where, pattern, index, xm, own, peer):
    slots = index.shape[0]
    return pl.pallas_call(
        finish_kernel,
        in_specs=[SMEM] * 3 + [VMEM] * 3,
        out_specs=[VMEM, HBM],
        out_shape=[
            jax.ShapeDtypeStruct((ROWS, COLS), jnp.bfloat16),
            jax.ShapeDtypeStruct((slots, BS, BS), jnp.bfloat16),
        ],
        scratch_shapes=[pltpu.VMEM((BLOCKS + 1, BS, BS), jnp.bfloat16), pltpu.SemaphoreType.DMA],
        compiler_params=pltpu.CompilerParams(vmem_limit_bytes=24 * 2**20),
        cost_estimate=pl.CostEstimate(flops=4 * ROWS * COLS, bytes_accessed=15 * 2**20, transcendentals=0),
        name="finish_payload",
    )(where, pattern, index, xm, own, peer)


FCH = 16


def force_kernel(d_ref, h_ref, s_ref, e_ref, out_ref):
    same = lax.broadcasted_iota(jnp.int32, (BS, BS), 0) == lax.broadcasted_iota(jnp.int32, (BS, BS), 1)
    ones = jnp.ones((BS, BS), jnp.bfloat16)
    for k in range(FCH):
        spread = jnp.where(same, e_ref[k : k + 1, :].astype(jnp.float32), 0.0).astype(jnp.bfloat16)
        energy = jnp.dot(spread, ones, preferred_element_type=jnp.float32)
        term = d_ref[k].astype(jnp.float32) * (
            h_ref[k].astype(jnp.float32) - energy * s_ref[k].astype(jnp.float32)
        )
        out_ref[k : k + 1, :] = jnp.sum(term, axis=0, keepdims=True)


def force_sums(dens, force_h, force_s, energy):
    slots = dens.shape[0]
    block = pl.BlockSpec((FCH, BS, BS), lambda i: (i, 0, 0))
    line = pl.BlockSpec((FCH, BS), lambda i: (i, 0))
    partial = pl.pallas_call(
        force_kernel,
        grid=(slots // FCH,),
        in_specs=[block, block, block, line],
        out_specs=line,
        out_shape=jax.ShapeDtypeStruct((slots, BS), jnp.float32),
        cost_estimate=pl.CostEstimate(
            flops=6 * slots * BS * BS, bytes_accessed=6 * slots * BS * BS, transcendentals=0
        ),
        name="force_sums",
    )(dens, force_h, force_s, energy)
    return jnp.sum(partial, axis=1)


def exchange(payload):
    return lax.all_to_all(payload, AXES, split_axis=0, concat_axis=0, tiled=True)


def shards(x, y, pattern_x, pattern_y, pattern_product, orbital_energy, pair_dest, pair_block, force_h, force_s):
    dest, wanted = pair_dest[0, :, 0], pair_block[0]
    slots = force_h.shape[0]
    entries = dest.shape[0]
    order = jnp.arange(entries, dtype=jnp.int32)
    earlier = (dest[:, None] == dest[None, :]) & (order[None, :] < order[:, None])
    rank = jnp.sum(earlier.astype(jnp.int32), axis=1)
    slot = dest * CAP + rank
    named = slot[None, :] == jnp.arange(slots, dtype=jnp.int32)[:, None]
    index = jnp.sum(jnp.where(named, wanted[None, :] - BLOCKS, 0), axis=1) + BLOCKS
    pick_row = (index[:, None] // QB == jnp.arange(RB, dtype=jnp.int32)[None, :]).astype(jnp.bfloat16)
    send_energy = jnp.dot(
        pick_row, orbital_energy.reshape(RB, BS), preferred_element_type=jnp.float32
    ).astype(jnp.bfloat16)

    where = jnp.stack([lax.axis_index(axis) for axis in AXES]).astype(jnp.int32)
    half, quarter = ROWS // 2, ROWS // 4
    y_peer = lax.ppermute(y, "c", SWAP)
    pattern_peer = lax.ppermute(pattern_y.T, "c", SWAP)
    xm = mask_x(x, pattern_x.T)
    ym = mask_y(y, y_peer, pattern_y.T, pattern_peer, where)

    xa_below = lax.ppermute(xm, "z", UP)
    xa_above = lax.ppermute(xm, "z", DOWN)
    xb_top = lax.ppermute(xm[:half], "yh", SWAP)
    ya_below = lax.ppermute(ym, "x", UP)
    ya_above = lax.ppermute(ym, "x", DOWN)
    yb = lax.ppermute(after(ym, xb_top), "yl", SWAP)
    energy = exchange(send_energy)

    xa_far = [lax.ppermute(xa_below[:half], "z", UP), lax.ppermute(xa_above[half:], "z", DOWN)]
    ya_far = [lax.ppermute(ya_below[:quarter], "x", UP), lax.ppermute(ya_above[quarter:], "x", DOWN)]
    xb_bottom = lax.ppermute(after(xm[half:], yb, energy), "yh", SWAP)

    xb_top_z = after(xb_top, *xa_far)
    xbt_below, xbt_above = lax.ppermute(xb_top_z, "z", UP), lax.ppermute(xb_top_z, "z", DOWN)
    yb_x = after(yb, *ya_far)
    yb_below, yb_above = lax.ppermute(yb_x, "x", UP), lax.ppermute(yb_x, "x", DOWN)
    xb_bottom_z = after(xb_bottom, xbt_below, xbt_above)
    xbb_below, xbb_above = lax.ppermute(xb_bottom_z, "z", UP), lax.ppermute(xb_bottom_z, "z", DOWN)

    xb_far = [
        lax.ppermute(after(xbt_below, xbb_below), "z", UP),
        lax.ppermute(xbb_above, "z", DOWN),
    ]
    yb_far = [lax.ppermute(yb_below[:quarter], "x", UP), lax.ppermute(yb_above[quarter:], "x", DOWN)]

    x_parts = [xm, xa_below, xa_above, *xa_far, xb_top, xb_bottom, xbt_below, xbb_below, xbt_above, xbb_above]
    y_parts = [ym, ya_below, ya_above, *ya_far, yb, yb_below, yb_above]
    own, far, x_late, y_late = early_product(x_parts, y_parts, where)
    own, far = late_product(where, xb_far, yb_far, x_late, y_late, own, far)
    peer = lax.ppermute(far, "c", SWAP)
    sign_next, payload = finish_and_payload(where, pattern_product.T, index, xm, own, peer)
    received = exchange(payload)
    return sign_next, force_sums(received, force_h, force_s, energy)


def solution(mesh):
    fine = Mesh(mesh.devices.reshape(2, 4, 2, 4, 2), AXES)
    row, col = ("yl", "x"), ("yh", "z", "c")
    in_specs = (
        P(row, col),
        P(row, col),
        P(row, col),
        P(row, col),
        P(row, col),
        P(row),
        P(AXES, None, None),
        P(AXES, None),
        P(AXES, None, None),
        P(AXES, None, None),
    )
    out_specs = (P(row, col), P(AXES))
    return jax.shard_map(shards, mesh=fine, in_specs=in_specs, out_specs=out_specs, check_vma=False)
```

```python
import jax
import jax.numpy as jnp
from jax import lax
from jax.experimental import pallas as pl
from jax.experimental.pallas import tpu as pltpu
from jax.sharding import Mesh, PartitionSpec as P

BS = 128
QB = 4
CAP = 2
RB = 8
BLOCKS = RB * QB
SEND = 32
ROWS = RB * BS
COLS = QB * BS
RING = 4
AXES = ("yl", "x", "yh", "z", "c")
SWAP = [(0, 1), (1, 0)]
UP = [(i, (i + 1) % RING) for i in range(RING)]
DOWN = [(i, (i - 1) % RING) for i in range(RING)]


def keep_block(pattern_ref, j, i):
    return (pattern_ref[j, i] > 0).astype(jnp.float32).astype(jnp.bfloat16)


def mask_x_kernel(p_ref, x_ref, o_ref, top_ref, bottom_ref):
    for i in range(RB):
        half_ref, shift = (top_ref, 0) if i < RB // 2 else (bottom_ref, RB // 2)
        for j in range(QB):
            rows, cols = slice(i * BS, (i + 1) * BS), slice(j * BS, (j + 1) * BS)
            kept = x_ref[rows, cols] * keep_block(p_ref, j, i)
            o_ref[rows, cols] = kept
            half_ref[slice((i - shift) * BS, (i - shift + 1) * BS), cols] = kept


def mask_y_kernel(where_ref, p_ref, q_ref, y_ref, z_ref, o_ref):
    first = where_ref[4] * (RB // 2)
    for i in range(RB // 2):
        rows = slice(i * BS, (i + 1) * BS)
        own_rows = pl.ds(pl.multiple_of((first + i) * BS, BS), BS)
        for j in range(QB):
            cols = slice(j * BS, (j + 1) * BS)
            far_cols = slice(COLS + j * BS, COLS + (j + 1) * BS)
            o_ref[rows, cols] = y_ref[own_rows, cols] * keep_block(p_ref, j, first + i)
            o_ref[rows, far_cols] = z_ref[own_rows, cols] * keep_block(q_ref, j, first + i)


SMEM = pl.BlockSpec(memory_space=pltpu.SMEM)
VMEM = pl.BlockSpec(memory_space=pltpu.VMEM)
HBM = pl.BlockSpec(memory_space=pltpu.HBM)


def mask_x(x, pattern):
    return pl.pallas_call(
        mask_x_kernel,
        in_specs=[SMEM, VMEM],
        out_specs=[VMEM] * 3,
        out_shape=[
            jax.ShapeDtypeStruct((ROWS, COLS), jnp.bfloat16),
            jax.ShapeDtypeStruct((ROWS // 2, COLS), jnp.bfloat16),
            jax.ShapeDtypeStruct((ROWS // 2, COLS), jnp.bfloat16),
        ],
        cost_estimate=pl.CostEstimate(flops=ROWS * COLS, bytes_accessed=6 * ROWS * COLS, transcendentals=0),
        name="mask_x",
    )(pattern, x)


def mask_y(y, y_peer, pattern, pattern_peer, where):
    return pl.pallas_call(
        mask_y_kernel,
        in_specs=[SMEM] * 3 + [VMEM] * 2,
        out_specs=VMEM,
        out_shape=jax.ShapeDtypeStruct((ROWS // 2, 2 * COLS), jnp.bfloat16),
        cost_estimate=pl.CostEstimate(flops=ROWS * COLS, bytes_accessed=4 * ROWS * COLS, transcendentals=0),
        name="mask_y",
    )(where, pattern, pattern_peer, y, y_peer)


def after(value, *others):
    return lax.optimization_barrier((value,) + others)[0]


def y_place(where_ref, position):
    yl, xi, yh, z = (where_ref[k] for k in range(4))
    member = position % 4
    offset = jnp.where(member == 0, 0, jnp.where(member == 1, 3, jnp.where(member == 2, 1, 2)))
    gap = (z + offset - xi + 2 * RING) % RING
    y_member = jnp.where(gap == 0, 0, jnp.where(gap == 3, 1, jnp.where(gap == 1, 2, 3)))
    return (yh ^ (position // 4) ^ yl) * 4 + y_member


X_PIECES = ((0, 0, 2), (1, 0, 2), (2, 0, 2), (3, 0, 1), (3, 1, 1), (4, 0, 1), (4, 1, 1), (5, 0, 1), (5, 1, 1), (6, 0, 1), (6, 1, 1))
Y_PIECES = ((0, 0, 2), (1, 0, 2), (2, 0, 2), (3, 0, 1), (3, 1, 1), (4, 0, 2), (5, 0, 2), (6, 0, 2))
EARLY = 7


def early_kernel(*refs):
    nx, ny = len(X_PIECES), len(Y_PIECES)
    x_in, y_in, where_ref = refs[:nx], refs[nx : nx + ny], refs[nx + ny]
    own_ref, far_ref, x_late, y_late = refs[nx + ny + 1 : nx + ny + 5]
    x_buf, y_buf, x_sem, y_sem = refs[nx + ny + 5 :]

    for k in range(max(nx, ny)):
        for pieces, source, buf, sem, half in (
            (X_PIECES, x_in, x_buf, x_sem, ROWS // 2),
            (Y_PIECES, y_in, y_buf, y_sem, ROWS // 4),
        ):
            if k < len(pieces):
                position, start, size = pieces[k]
                target = buf.at[position, pl.ds(start * half, size * half)]
                pltpu.make_async_copy(source[k], target, sem.at[position]).start()

    own_ref[...] = jnp.zeros_like(own_ref)
    far_ref[...] = jnp.zeros_like(far_ref)

    def step(position, carry):
        pltpu.make_async_copy(x_buf.at[position], x_buf.at[position], x_sem.at[position]).wait()
        y_position = y_place(where_ref, position)

        @pl.when(y_position != EARLY)
        def _():
            pltpu.make_async_copy(y_buf.at[y_position], y_buf.at[y_position], y_sem.at[y_position]).wait()
            for out_ref, cols in ((own_ref, slice(0, COLS)), (far_ref, slice(COLS, 2 * COLS))):
                out_ref[...] += jnp.dot(
                    x_buf[position], y_buf[y_position, :, cols], preferred_element_type=jnp.float32
                )

        @pl.when(y_position == EARLY)
        def _():
            x_late[...] = x_buf[position]

        return carry

    lax.fori_loop(0, EARLY, step, 0)
    last = y_place(where_ref, EARLY)

    @pl.when(last != EARLY)
    def _():
        pltpu.make_async_copy(y_buf.at[last], y_buf.at[last], y_sem.at[last]).wait()
        y_late[...] = y_buf[last]


def early_product(x_parts, y_parts, where):
    return pl.pallas_call(
        early_kernel,
        in_specs=[HBM] * (len(X_PIECES) + len(Y_PIECES)) + [SMEM],
        out_specs=[VMEM] * 4,
        out_shape=[
            jax.ShapeDtypeStruct((ROWS, COLS), jnp.float32),
            jax.ShapeDtypeStruct((ROWS, COLS), jnp.float32),
            jax.ShapeDtypeStruct((ROWS, COLS), jnp.bfloat16),
            jax.ShapeDtypeStruct((ROWS // 2, 2 * COLS), jnp.bfloat16),
        ],
        scratch_shapes=[
            pltpu.VMEM((EARLY, ROWS, COLS), jnp.bfloat16),
            pltpu.VMEM((EARLY, ROWS // 2, 2 * COLS), jnp.bfloat16),
            pltpu.SemaphoreType.DMA((EARLY,)),
            pltpu.SemaphoreType.DMA((EARLY,)),
        ],
        compiler_params=pltpu.CompilerParams(vmem_limit_bytes=24 * 2**20),
        cost_estimate=pl.CostEstimate(
            flops=14 * ROWS * COLS * ROWS, bytes_accessed=20 * 2**20, transcendentals=0
        ),
        name="early_product",
    )(*x_parts, *y_parts, where)


def late_kernel(where_ref, x_top, x_bottom, y_top, y_bottom, x_late, y_late, own_ref, far_ref, own_out, far_out):
    last = y_place(where_ref, EARLY)
    quarter = ROWS // 4

    def add(x_far, same_chunk):
        x_last = x_far if same_chunk else x_late
        for sum_ref, out_ref, cols in (
            (own_ref, own_out, slice(0, COLS)),
            (far_ref, far_out, slice(COLS, 2 * COLS)),
        ):
            total = sum_ref[...]
            total += jnp.dot(x_last[:, :quarter], y_top[:, cols], preferred_element_type=jnp.float32)
            total += jnp.dot(x_last[:, quarter:], y_bottom[:, cols], preferred_element_type=jnp.float32)
            if not same_chunk:
                total += jnp.dot(x_far[...], y_late[:, cols], preferred_element_type=jnp.float32)
            out_ref[...] = total

    for upper, x_far in ((True, x_top), (False, x_bottom)):
        for same_chunk in (True, False):
            here = (pl.program_id(0) < 2) == upper
            pl.when(here & ((last == EARLY) == same_chunk))(lambda x=x_far, t=same_chunk: add(x, t))


def late_product(where, x_far, y_far, x_late, y_late, own, far):
    quarter = ROWS // 4
    top = pl.BlockSpec((quarter, COLS), lambda m: (jnp.minimum(m, 1), 0))
    bottom = pl.BlockSpec((quarter, COLS), lambda m: (jnp.maximum(m - 2, 0), 0))
    rows = pl.BlockSpec((quarter, COLS), lambda m: (m, 0))

    def whole(height):
        return pl.BlockSpec((height, 2 * COLS), lambda m: (0, 0))

    return pl.pallas_call(
        late_kernel,
        grid=(4,),
        in_specs=[SMEM, top, bottom, whole(quarter), whole(quarter), rows, whole(2 * quarter), rows, rows],
        out_specs=[rows] * 2,
        out_shape=[jax.ShapeDtypeStruct((ROWS, COLS), jnp.float32)] * 2,
        compiler_params=pltpu.CompilerParams(vmem_limit_bytes=24 * 2**20),
        cost_estimate=pl.CostEstimate(
            flops=4 * ROWS * COLS * ROWS, bytes_accessed=12 * 2**20, transcendentals=0
        ),
        name="late_product",
    )(where, *x_far, *y_far, x_late, y_late, own, far)


def finish_kernel(where_ref, pattern_ref, index_ref, xm_ref, own_ref, peer_ref, sign_ref, payload_ref, dens, stage, out_sem):
    yl, xi, yh, z, core = (where_ref[k] for k in range(5))
    block_row = (yl * 4 + xi) * RB
    block_col = ((yh * 4 + z) * 2 + core) * QB
    same = lax.broadcasted_iota(jnp.int32, (BS, BS), 0) == lax.broadcasted_iota(jnp.int32, (BS, BS), 1)
    half_eye = jnp.where(same, 0.5, 0.0).astype(jnp.float32)

    def finish(i, carry):
        rows = pl.ds(pl.multiple_of(i * BS, BS), BS)
        for j in range(QB):
            cols = slice(j * BS, (j + 1) * BS)
            kept = jnp.where(pattern_ref[j, i] > 0, 0.5, 0.0)
            product = own_ref[rows, cols] + peer_ref[rows, cols]
            xnew = 1.5 * xm_ref[rows, cols].astype(jnp.float32) - kept * product
            sign_ref[rows, cols] = xnew.astype(jnp.bfloat16)
            on_diagonal = jnp.where(block_row + i == block_col + j, 1.0, 0.0)
            dens[i * QB + j] = (on_diagonal * half_eye - 0.5 * xnew).astype(jnp.bfloat16)
        return carry

    lax.fori_loop(0, RB, finish, 0)
    dens[BLOCKS] = jnp.zeros((BS, BS), jnp.bfloat16)

    chunks = stage.shape[0] // SEND

    def copy(slot, carry):
        stage[slot] = dens[index_ref[slot]]
        return carry

    for chunk in range(chunks):
        lax.fori_loop(chunk * SEND, (chunk + 1) * SEND, copy, 0, unroll=8)
        part = pl.ds(chunk * SEND, SEND)
        pltpu.make_async_copy(stage.at[part], payload_ref.at[part], out_sem.at[chunk]).start()
    for chunk in range(chunks):
        part = pl.ds(chunk * SEND, SEND)
        pltpu.make_async_copy(stage.at[part], payload_ref.at[part], out_sem.at[chunk]).wait()


def finish_and_payload(where, pattern, index, xm, own, peer):
    slots = index.shape[0]
    return pl.pallas_call(
        finish_kernel,
        in_specs=[SMEM] * 3 + [VMEM] * 3,
        out_specs=[VMEM, HBM],
        out_shape=[
            jax.ShapeDtypeStruct((ROWS, COLS), jnp.bfloat16),
            jax.ShapeDtypeStruct((slots, BS, BS), jnp.bfloat16),
        ],
        scratch_shapes=[
            pltpu.VMEM((BLOCKS + 1, BS, BS), jnp.bfloat16),
            pltpu.VMEM((slots, BS, BS), jnp.bfloat16),
            pltpu.SemaphoreType.DMA((slots // SEND,)),
        ],
        compiler_params=pltpu.CompilerParams(vmem_limit_bytes=24 * 2**20),
        cost_estimate=pl.CostEstimate(flops=4 * ROWS * COLS, bytes_accessed=15 * 2**20, transcendentals=0),
        name="finish_payload",
    )(where, pattern, index, xm, own, peer)


FCH = 32


def force_kernel(d_ref, h_ref, s_ref, e_ref, out_ref):
    same = lax.broadcasted_iota(jnp.int32, (BS, BS), 0) == lax.broadcasted_iota(jnp.int32, (BS, BS), 1)
    ones = jnp.ones((BS, BS), jnp.bfloat16)
    for k in range(FCH):
        spread = jnp.where(same, e_ref[k : k + 1, :].astype(jnp.float32), 0.0).astype(jnp.bfloat16)
        energy = jnp.dot(spread, ones, preferred_element_type=jnp.float32)
        term = d_ref[k].astype(jnp.float32) * (
            h_ref[k].astype(jnp.float32) - energy * s_ref[k].astype(jnp.float32)
        )
        out_ref[k : k + 1, :] = jnp.sum(term, axis=0, keepdims=True)


def force_sums(dens, force_h, force_s, energy):
    slots = dens.shape[0]
    block = pl.BlockSpec((FCH, BS, BS), lambda i: (i, 0, 0))
    line = pl.BlockSpec((FCH, BS), lambda i: (i, 0))
    partial = pl.pallas_call(
        force_kernel,
        grid=(slots // FCH,),
        in_specs=[block, block, block, line],
        out_specs=line,
        out_shape=jax.ShapeDtypeStruct((slots, BS), jnp.float32),
        compiler_params=pltpu.CompilerParams(vmem_limit_bytes=24 * 2**20),
        cost_estimate=pl.CostEstimate(
            flops=6 * slots * BS * BS, bytes_accessed=6 * slots * BS * BS, transcendentals=0
        ),
        name="force_sums",
    )(dens, force_h, force_s, energy)
    return jnp.sum(partial, axis=1)


def exchange(payload):
    return lax.all_to_all(payload, AXES, split_axis=0, concat_axis=0, tiled=True)


def shards(x, y, pattern_x, pattern_y, pattern_product, orbital_energy, pair_dest, pair_block, force_h, force_s):
    dest, wanted = pair_dest[0, :, 0], pair_block[0]
    slots = force_h.shape[0]
    entries = dest.shape[0]
    order = jnp.arange(entries, dtype=jnp.int32)
    earlier = (dest[:, None] == dest[None, :]) & (order[None, :] < order[:, None])
    rank = jnp.sum(earlier.astype(jnp.int32), axis=1)
    slot = dest * CAP + rank
    named = slot[None, :] == jnp.arange(slots, dtype=jnp.int32)[:, None]
    index = jnp.sum(jnp.where(named, wanted[None, :] - BLOCKS, 0), axis=1) + BLOCKS
    pick_row = (index[:, None] // QB == jnp.arange(RB, dtype=jnp.int32)[None, :]).astype(jnp.bfloat16)
    send_energy = jnp.dot(
        pick_row, orbital_energy.reshape(RB, BS), preferred_element_type=jnp.float32
    ).astype(jnp.bfloat16)

    where = jnp.stack([lax.axis_index(axis) for axis in AXES]).astype(jnp.int32)
    half, quarter = ROWS // 2, ROWS // 4
    y_peer = lax.ppermute(y, "c", SWAP)
    pattern_peer = lax.ppermute(pattern_y.T, "c", SWAP)
    xm, xm_top, xm_bottom = mask_x(x, pattern_x.T)
    ym = mask_y(y, y_peer, pattern_y.T, pattern_peer, where)

    ya_below = lax.ppermute(ym, "x", UP)
    ya_above = lax.ppermute(ym, "x", DOWN)
    yb = lax.ppermute(ym, "yl", SWAP)
    xm_z = after(xm, ym)
    xa_below = lax.ppermute(xm_z, "z", UP)
    xa_above = lax.ppermute(xm_z, "z", DOWN)
    energy = exchange(after(send_energy, xm, ym))

    xa_below, xa_above, ya_below, ya_above, yb, energy = lax.optimization_barrier(
        (xa_below, xa_above, ya_below, ya_above, yb, energy)
    )
    xa_far = [lax.ppermute(xa_below[:half], "z", UP), lax.ppermute(xa_above[half:], "z", DOWN)]
    ya_far = [lax.ppermute(ya_below[:quarter], "x", UP), lax.ppermute(ya_above[quarter:], "x", DOWN)]
    xb_top = lax.ppermute(after(xm_top, yb), "yh", SWAP)
    xb_bottom = lax.ppermute(after(xm_bottom, xb_top), "yh", SWAP)

    xb_top_z = after(xb_top, *xa_far)
    xbt_below, xbt_above = lax.ppermute(xb_top_z, "z", UP), lax.ppermute(xb_top_z, "z", DOWN)
    yb_x = after(yb, *ya_far)
    yb_below, yb_above = lax.ppermute(yb_x, "x", UP), lax.ppermute(yb_x, "x", DOWN)
    xb_bottom_z = after(xb_bottom, xbt_below, xbt_above)
    xbb_below, xbb_above = lax.ppermute(xb_bottom_z, "z", UP), lax.ppermute(xb_bottom_z, "z", DOWN)

    xb_far = [
        lax.ppermute(after(xbt_below, xbb_below), "z", UP),
        lax.ppermute(xbb_above, "z", DOWN),
    ]
    yb_far = [lax.ppermute(yb_below[:quarter], "x", UP), lax.ppermute(yb_above[quarter:], "x", DOWN)]

    x_parts = [xm, xa_below, xa_above, *xa_far, xb_top, xb_bottom, xbt_below, xbb_below, xbt_above, xbb_above]
    y_parts = [ym, ya_below, ya_above, *ya_far, yb, yb_below, yb_above]
    own, far, x_late, y_late = early_product(x_parts, y_parts, where)
    own, far = late_product(where, xb_far, yb_far, x_late, y_late, own, far)
    peer = lax.ppermute(far, "c", SWAP)
    sign_next, payload = finish_and_payload(where, pattern_product.T, index, xm, own, peer)
    received = exchange(payload)
    return sign_next, force_sums(received, force_h, force_s, energy)


def solution(mesh):
    fine = Mesh(mesh.devices.reshape(2, 4, 2, 4, 2), AXES)
    row, col = ("yl", "x"), ("yh", "z", "c")
    in_specs = (
        P(row, col),
        P(row, col),
        P(row, col),
        P(row, col),
        P(row, col),
        P(row),
        P(AXES, None, None),
        P(AXES, None),
        P(AXES, None, None),
        P(AXES, None, None),
    )
    out_specs = (P(row, col), P(AXES))
    return jax.shard_map(shards, mesh=fine, in_specs=in_specs, out_specs=out_specs, check_vma=False)
```

```python
import jax
import jax.numpy as jnp
from jax import lax
from jax.experimental import pallas as pl
from jax.experimental.pallas import tpu as pltpu
from jax.sharding import Mesh, PartitionSpec as P

BS = 128
QB = 4
CAP = 2
RB = 8
BLOCKS = RB * QB
SEND = 16
TAIL = 8
ROWS = RB * BS
COLS = QB * BS
RING = 4
AXES = ("yl", "x", "yh", "z", "c")
SWAP = [(0, 1), (1, 0)]
UP = [(i, (i + 1) % RING) for i in range(RING)]
DOWN = [(i, (i - 1) % RING) for i in range(RING)]


def keep_block(pattern_ref, j, i):
    return (pattern_ref[j, i] > 0).astype(jnp.float32).astype(jnp.bfloat16)


def mask_kernel(
    where_ref, px_ref, py_ref, pz_ref, x_hbm, y_hbm, z_ref, xo_ref, top_ref, bottom_ref, yo_ref, x_ref, y_ref, sem
):
    first = where_ref[4] * (RB // 2)
    own_rows = pl.ds(pl.multiple_of(first * BS, ROWS // 2), ROWS // 2)
    x_copy = pltpu.make_async_copy(x_hbm, x_ref, sem.at[0])
    y_copy = pltpu.make_async_copy(y_hbm.at[own_rows], y_ref, sem.at[1])
    x_copy.start()
    y_copy.start()
    x_copy.wait()
    for i in range(RB):
        half_ref, shift = (top_ref, 0) if i < RB // 2 else (bottom_ref, RB // 2)
        for j in range(QB):
            rows, cols = slice(i * BS, (i + 1) * BS), slice(j * BS, (j + 1) * BS)
            kept = x_ref[rows, cols] * keep_block(px_ref, j, i)
            xo_ref[rows, cols] = kept
            half_ref[slice((i - shift) * BS, (i - shift + 1) * BS), cols] = kept
    y_copy.wait()
    for i in range(RB // 2):
        rows = slice(i * BS, (i + 1) * BS)
        peer_rows = pl.ds(pl.multiple_of((first + i) * BS, BS), BS)
        for j in range(QB):
            cols = slice(j * BS, (j + 1) * BS)
            far_cols = slice(COLS + j * BS, COLS + (j + 1) * BS)
            yo_ref[rows, cols] = y_ref[rows, cols] * keep_block(py_ref, j, first + i)
            yo_ref[rows, far_cols] = z_ref[peer_rows, cols] * keep_block(pz_ref, j, first + i)


SMEM = pl.BlockSpec(memory_space=pltpu.SMEM)
VMEM = pl.BlockSpec(memory_space=pltpu.VMEM)
HBM = pl.BlockSpec(memory_space=pltpu.HBM)


def masked_tiles(where, pattern_x, pattern_y, pattern_peer, x, y, y_peer):
    half = jax.ShapeDtypeStruct((ROWS // 2, COLS), jnp.bfloat16)
    return pl.pallas_call(
        mask_kernel,
        in_specs=[SMEM] * 4 + [HBM] * 2 + [VMEM],
        out_specs=[VMEM] * 4,
        out_shape=[
            jax.ShapeDtypeStruct((ROWS, COLS), jnp.bfloat16),
            half,
            half,
            jax.ShapeDtypeStruct((ROWS // 2, 2 * COLS), jnp.bfloat16),
        ],
        scratch_shapes=[
            pltpu.VMEM((ROWS, COLS), jnp.bfloat16),
            pltpu.VMEM((ROWS // 2, COLS), jnp.bfloat16),
            pltpu.SemaphoreType.DMA((2,)),
        ],
        compiler_params=pltpu.CompilerParams(vmem_limit_bytes=12 * 2**20),
        cost_estimate=pl.CostEstimate(flops=2 * ROWS * COLS, bytes_accessed=12 * ROWS * COLS, transcendentals=0),
        name="mask_tiles",
    )(where, pattern_x, pattern_y, pattern_peer, x, y, y_peer)


def after(value, *others):
    return lax.optimization_barrier((value,) + others)[0]


def y_place(where_ref, position):
    yl, xi, yh, z = (where_ref[k] for k in range(4))
    member = position % 4
    offset = jnp.where(member == 0, 0, jnp.where(member == 1, 3, jnp.where(member == 2, 1, 2)))
    gap = (z + offset - xi + 2 * RING) % RING
    y_member = jnp.where(gap == 0, 0, jnp.where(gap == 3, 1, jnp.where(gap == 1, 2, 3)))
    return (yh ^ (position // 4) ^ yl) * 4 + y_member


X_PIECES = ((0, 0, 2), (1, 0, 2), (2, 0, 2), (3, 0, 1), (3, 1, 1), (4, 0, 1), (4, 1, 1), (5, 0, 1), (5, 1, 1), (6, 0, 1), (6, 1, 1))
Y_PIECES = ((0, 0, 2), (1, 0, 2), (2, 0, 2), (3, 0, 1), (3, 1, 1), (4, 0, 2), (5, 0, 2), (6, 0, 2))
EARLY = 7


def early_kernel(*refs):
    nx, ny = len(X_PIECES), len(Y_PIECES)
    x_in, y_in, where_ref = refs[:nx], refs[nx : nx + ny], refs[nx + ny]
    own_ref, far_ref, x_late, y_late = refs[nx + ny + 1 : nx + ny + 5]
    x_buf, y_buf, x_sem, y_sem = refs[nx + ny + 5 :]

    for k in range(max(nx, ny)):
        for pieces, source, buf, sem, half in (
            (X_PIECES, x_in, x_buf, x_sem, ROWS // 2),
            (Y_PIECES, y_in, y_buf, y_sem, ROWS // 4),
        ):
            if k < len(pieces):
                position, start, size = pieces[k]
                target = buf.at[position, pl.ds(start * half, size * half)]
                pltpu.make_async_copy(source[k], target, sem.at[position]).start()

    own_ref[...] = jnp.zeros_like(own_ref)
    far_ref[...] = jnp.zeros_like(far_ref)

    def step(position, carry):
        pltpu.make_async_copy(x_buf.at[position], x_buf.at[position], x_sem.at[position]).wait()
        y_position = y_place(where_ref, position)

        @pl.when(y_position != EARLY)
        def _():
            pltpu.make_async_copy(y_buf.at[y_position], y_buf.at[y_position], y_sem.at[y_position]).wait()
            for out_ref, cols in ((own_ref, slice(0, COLS)), (far_ref, slice(COLS, 2 * COLS))):
                out_ref[...] += jnp.dot(
                    x_buf[position], y_buf[y_position, :, cols], preferred_element_type=jnp.float32
                )

        @pl.when(y_position == EARLY)
        def _():
            x_late[...] = x_buf[position]

        return carry

    lax.fori_loop(0, EARLY, step, 0)
    last = y_place(where_ref, EARLY)

    @pl.when(last != EARLY)
    def _():
        pltpu.make_async_copy(y_buf.at[last], y_buf.at[last], y_sem.at[last]).wait()
        y_late[...] = y_buf[last]


def early_product(x_parts, y_parts, where):
    return pl.pallas_call(
        early_kernel,
        in_specs=[HBM] * (len(X_PIECES) + len(Y_PIECES)) + [SMEM],
        out_specs=[VMEM] * 4,
        out_shape=[
            jax.ShapeDtypeStruct((ROWS, COLS), jnp.float32),
            jax.ShapeDtypeStruct((ROWS, COLS), jnp.float32),
            jax.ShapeDtypeStruct((ROWS, COLS), jnp.bfloat16),
            jax.ShapeDtypeStruct((ROWS // 2, 2 * COLS), jnp.bfloat16),
        ],
        scratch_shapes=[
            pltpu.VMEM((EARLY, ROWS, COLS), jnp.bfloat16),
            pltpu.VMEM((EARLY, ROWS // 2, 2 * COLS), jnp.bfloat16),
            pltpu.SemaphoreType.DMA((EARLY,)),
            pltpu.SemaphoreType.DMA((EARLY,)),
        ],
        compiler_params=pltpu.CompilerParams(vmem_limit_bytes=24 * 2**20),
        cost_estimate=pl.CostEstimate(
            flops=14 * ROWS * COLS * ROWS, bytes_accessed=20 * 2**20, transcendentals=0
        ),
        name="early_product",
    )(*x_parts, *y_parts, where)


def late_kernel(where_ref, x_top, x_bottom, y_top, y_bottom, x_late, y_late, own_ref, far_ref, own_out, far_out):
    last = y_place(where_ref, EARLY)
    quarter = ROWS // 4

    def add(x_far, same_chunk):
        x_last = x_far if same_chunk else x_late
        for sum_ref, out_ref, cols in (
            (own_ref, own_out, slice(0, COLS)),
            (far_ref, far_out, slice(COLS, 2 * COLS)),
        ):
            total = sum_ref[...]
            total += jnp.dot(x_last[:, :quarter], y_top[:, cols], preferred_element_type=jnp.float32)
            total += jnp.dot(x_last[:, quarter:], y_bottom[:, cols], preferred_element_type=jnp.float32)
            if not same_chunk:
                total += jnp.dot(x_far[...], y_late[:, cols], preferred_element_type=jnp.float32)
            out_ref[...] = total

    for upper, x_far in ((True, x_top), (False, x_bottom)):
        for same_chunk in (True, False):
            here = (pl.program_id(0) < 2) == upper
            pl.when(here & ((last == EARLY) == same_chunk))(lambda x=x_far, t=same_chunk: add(x, t))


def late_product(where, x_far, y_far, x_late, y_late, own, far):
    quarter = ROWS // 4
    top = pl.BlockSpec((quarter, COLS), lambda m: (jnp.minimum(m, 1), 0))
    bottom = pl.BlockSpec((quarter, COLS), lambda m: (jnp.maximum(m - 2, 0), 0))
    rows = pl.BlockSpec((quarter, COLS), lambda m: (m, 0))

    def whole(height):
        return pl.BlockSpec((height, 2 * COLS), lambda m: (0, 0))

    return pl.pallas_call(
        late_kernel,
        grid=(4,),
        in_specs=[SMEM, top, bottom, whole(quarter), whole(quarter), rows, whole(2 * quarter), rows, rows],
        out_specs=[rows] * 2,
        out_shape=[jax.ShapeDtypeStruct((ROWS, COLS), jnp.float32)] * 2,
        compiler_params=pltpu.CompilerParams(vmem_limit_bytes=24 * 2**20),
        cost_estimate=pl.CostEstimate(
            flops=4 * ROWS * COLS * ROWS, bytes_accessed=12 * 2**20, transcendentals=0
        ),
        name="late_product",
    )(where, *x_far, *y_far, x_late, y_late, own, far)


def finish_kernel(where_ref, pattern_ref, index_ref, energy_ref, xm_ref, own_ref, peer_ref, sign_ref, payload_ref, dens, stage, out_sem):
    yl, xi, yh, z, core = (where_ref[k] for k in range(5))
    block_row = (yl * 4 + xi) * RB
    block_col = ((yh * 4 + z) * 2 + core) * QB
    same = lax.broadcasted_iota(jnp.int32, (BS, BS), 0) == lax.broadcasted_iota(jnp.int32, (BS, BS), 1)
    half_eye = jnp.where(same, 0.5, 0.0).astype(jnp.float32)

    def finish(i, carry):
        rows = pl.ds(pl.multiple_of(i * BS, BS), BS)
        for j in range(QB):
            cols = slice(j * BS, (j + 1) * BS)
            kept = jnp.where(pattern_ref[j, i] > 0, 0.5, 0.0)
            product = own_ref[rows, cols] + peer_ref[rows, cols]
            xnew = 1.5 * xm_ref[rows, cols].astype(jnp.float32) - kept * product
            sign_ref[rows, cols] = xnew.astype(jnp.bfloat16)
            on_diagonal = jnp.where(block_row + i == block_col + j, 1.0, 0.0)
            dens[i * QB + j] = (on_diagonal * half_eye - 0.5 * xnew).astype(jnp.bfloat16)
        return carry

    lax.fori_loop(0, RB, finish, 0)
    dens[BLOCKS] = jnp.zeros((BS, BS), jnp.bfloat16)

    chunks = stage.shape[0] // SEND
    line = lax.broadcasted_iota(jnp.int32, (TAIL, BS), 0)

    def copy(owner, carry):
        energies = jnp.zeros((TAIL, BS), jnp.float32)
        for k in range(CAP):
            block = index_ref[owner * CAP + k]
            stage[owner, k * BS : (k + 1) * BS, :] = dens[block]
            energies = jnp.where(line == k, energy_ref[block // QB], energies)
        stage[owner, CAP * BS :, :] = energies.astype(jnp.bfloat16)
        return carry

    for chunk in range(chunks):
        lax.fori_loop(chunk * SEND, (chunk + 1) * SEND, copy, 0, unroll=4)
        part = pl.ds(chunk * SEND, SEND)
        pltpu.make_async_copy(stage.at[part], payload_ref.at[part], out_sem.at[chunk]).start()
    for chunk in range(chunks):
        part = pl.ds(chunk * SEND, SEND)
        pltpu.make_async_copy(stage.at[part], payload_ref.at[part], out_sem.at[chunk]).wait()


def finish_and_payload(where, pattern, index, energy, xm, own, peer):
    owners = index.shape[0] // CAP
    packet = (owners, CAP * BS + TAIL, BS)
    return pl.pallas_call(
        finish_kernel,
        in_specs=[SMEM] * 3 + [VMEM] * 4,
        out_specs=[VMEM, HBM],
        out_shape=[
            jax.ShapeDtypeStruct((ROWS, COLS), jnp.bfloat16),
            jax.ShapeDtypeStruct(packet, jnp.bfloat16),
        ],
        scratch_shapes=[
            pltpu.VMEM((BLOCKS + 1, BS, BS), jnp.bfloat16),
            pltpu.VMEM(packet, jnp.bfloat16),
            pltpu.SemaphoreType.DMA((owners // SEND,)),
        ],
        compiler_params=pltpu.CompilerParams(vmem_limit_bytes=18 * 2**20),
        cost_estimate=pl.CostEstimate(flops=4 * ROWS * COLS, bytes_accessed=15 * 2**20, transcendentals=0),
        name="finish_payload",
    )(where, pattern, index, energy, xm, own, peer)


FCH = 16


def force_kernel(d_ref, h_ref, s_ref, out_ref):
    same = lax.broadcasted_iota(jnp.int32, (BS, BS), 0) == lax.broadcasted_iota(jnp.int32, (BS, BS), 1)
    ones = jnp.ones((BS, BS), jnp.bfloat16)
    for source in range(FCH):
        energies = d_ref[source, CAP * BS :, :].astype(jnp.float32)
        for k in range(CAP):
            slot = source * CAP + k
            spread = jnp.where(same, energies[k : k + 1, :], 0.0).astype(jnp.bfloat16)
            energy = jnp.dot(spread, ones, preferred_element_type=jnp.float32)
            term = d_ref[source, k * BS : (k + 1) * BS, :].astype(jnp.float32) * (
                h_ref[slot].astype(jnp.float32) - energy * s_ref[slot].astype(jnp.float32)
            )
            out_ref[slot : slot + 1, :] = jnp.sum(term, axis=0, keepdims=True)


def force_sums(packets, force_h, force_s):
    slots = force_h.shape[0]
    block = pl.BlockSpec((FCH * CAP, BS, BS), lambda i: (i, 0, 0))
    partial = pl.pallas_call(
        force_kernel,
        grid=(slots // (FCH * CAP),),
        in_specs=[pl.BlockSpec((FCH, CAP * BS + TAIL, BS), lambda i: (i, 0, 0)), block, block],
        out_specs=pl.BlockSpec((FCH * CAP, BS), lambda i: (i, 0)),
        out_shape=jax.ShapeDtypeStruct((slots, BS), jnp.float32),
        compiler_params=pltpu.CompilerParams(vmem_limit_bytes=12 * 2**20),
        cost_estimate=pl.CostEstimate(
            flops=6 * slots * BS * BS, bytes_accessed=6 * slots * BS * BS, transcendentals=0
        ),
        name="force_sums",
    )(packets, force_h, force_s)
    return jnp.sum(partial, axis=1)


def exchange(payload):
    return lax.all_to_all(payload, AXES, split_axis=0, concat_axis=0, tiled=True)


def shards(x, y, pattern_x, pattern_y, pattern_product, orbital_energy, pair_dest, pair_block, force_h, force_s):
    dest, wanted = pair_dest[0, :, 0], pair_block[0]
    slots = force_h.shape[0]
    entries = dest.shape[0]
    order = jnp.arange(entries, dtype=jnp.int32)
    earlier = (dest[:, None] == dest[None, :]) & (order[None, :] < order[:, None])
    rank = jnp.sum(earlier.astype(jnp.int32), axis=1)
    slot = dest * CAP + rank
    named = slot[None, :] == jnp.arange(slots, dtype=jnp.int32)[:, None]
    index = jnp.sum(jnp.where(named, wanted[None, :] - BLOCKS, 0), axis=1) + BLOCKS
    energy = jnp.pad(orbital_energy.astype(jnp.float32).reshape(RB, 1, BS), ((0, 1), (0, 0), (0, 0)))

    where = jnp.stack([lax.axis_index(axis) for axis in AXES]).astype(jnp.int32)
    half, quarter = ROWS // 2, ROWS // 4
    y_peer = lax.ppermute(y, "c", SWAP)
    pattern_peer = lax.ppermute(pattern_y.T, "c", SWAP)
    xm, xm_top, xm_bottom, ym = masked_tiles(
        where, pattern_x.T, pattern_y.T, pattern_peer, x, y, y_peer
    )

    xb_top = lax.ppermute(xm_top, "yh", SWAP)
    xa_below = lax.ppermute(xm, "z", UP)
    xa_above = lax.ppermute(xm, "z", DOWN)
    ya_below = lax.ppermute(ym, "x", UP)
    ya_above = lax.ppermute(ym, "x", DOWN)
    yb = lax.ppermute(after(ym, xb_top), "yl", SWAP)
    xb_bottom = lax.ppermute(after(xm_bottom, yb), "yh", SWAP)

    xa_far = [lax.ppermute(xa_below[:half], "z", UP), lax.ppermute(xa_above[half:], "z", DOWN)]
    ya_far = [lax.ppermute(ya_below[:quarter], "x", UP), lax.ppermute(ya_above[quarter:], "x", DOWN)]

    xb_top_z = after(xb_top, *xa_far)
    xbt_below, xbt_above = lax.ppermute(xb_top_z, "z", UP), lax.ppermute(xb_top_z, "z", DOWN)
    yb_x = after(yb, *ya_far)
    yb_below, yb_above = lax.ppermute(yb_x, "x", UP), lax.ppermute(yb_x, "x", DOWN)
    xb_bottom_z = after(xb_bottom, xbt_below, xbt_above)
    xbb_below, xbb_above = lax.ppermute(xb_bottom_z, "z", UP), lax.ppermute(xb_bottom_z, "z", DOWN)

    xb_far = [
        lax.ppermute(after(xbt_below, xbb_below), "z", UP),
        lax.ppermute(xbb_above, "z", DOWN),
    ]
    yb_far = [lax.ppermute(yb_below[:quarter], "x", UP), lax.ppermute(yb_above[quarter:], "x", DOWN)]

    x_parts = [xm, xa_below, xa_above, *xa_far, xb_top, xb_bottom, xbt_below, xbb_below, xbt_above, xbb_above]
    y_parts = [ym, ya_below, ya_above, *ya_far, yb, yb_below, yb_above]
    own, far, x_late, y_late = early_product(x_parts, y_parts, where)
    own, far = late_product(where, xb_far, yb_far, x_late, y_late, own, far)
    peer = lax.ppermute(far, "c", SWAP)
    sign_next, payload = finish_and_payload(where, pattern_product.T, index, energy, xm, own, peer)
    received = exchange(payload)
    return sign_next, force_sums(received, force_h, force_s)


def solution(mesh):
    fine = Mesh(mesh.devices.reshape(2, 4, 2, 4, 2), AXES)
    row, col = ("yl", "x"), ("yh", "z", "c")
    in_specs = (
        P(row, col),
        P(row, col),
        P(row, col),
        P(row, col),
        P(row, col),
        P(row),
        P(AXES, None, None),
        P(AXES, None),
        P(AXES, None, None),
        P(AXES, None, None),
    )
    out_specs = (P(row, col), P(AXES))
    return jax.shard_map(shards, mesh=fine, in_specs=in_specs, out_specs=out_specs, check_vma=False)
```

```python
import jax
import jax.numpy as jnp
from jax import lax
from jax.experimental import pallas as pl
from jax.experimental.pallas import tpu as pltpu
from jax.sharding import Mesh, PartitionSpec as P

BS = 128
QB = 4
CAP = 2
RB = 8
BLOCKS = RB * QB
TAIL = 8
ROWS = RB * BS
COLS = QB * BS
RING = 4
AXES = ("yl", "x", "yh", "z", "c")
SWAP = [(0, 1), (1, 0)]
UP = [(i, (i + 1) % RING) for i in range(RING)]
DOWN = [(i, (i - 1) % RING) for i in range(RING)]


def keep_block(pattern_ref, j, i):
    return (pattern_ref[j, i] > 0).astype(jnp.float32).astype(jnp.bfloat16)


def mask_x_kernel(p_ref, x_ref, o_ref):
    for i in range(RB):
        for j in range(QB):
            rows, cols = slice(i * BS, (i + 1) * BS), slice(j * BS, (j + 1) * BS)
            o_ref[rows, cols] = x_ref[rows, cols] * keep_block(p_ref, j, i)


def mask_y_kernel(where_ref, p_ref, q_ref, y_ref, z_ref, o_ref):
    first = where_ref[4] * (RB // 2)
    for i in range(RB // 2):
        rows = slice(i * BS, (i + 1) * BS)
        own_rows = pl.ds(pl.multiple_of((first + i) * BS, BS), BS)
        for j in range(QB):
            cols = slice(j * BS, (j + 1) * BS)
            far_cols = slice(COLS + j * BS, COLS + (j + 1) * BS)
            o_ref[rows, cols] = y_ref[own_rows, cols] * keep_block(p_ref, j, first + i)
            o_ref[rows, far_cols] = z_ref[own_rows, cols] * keep_block(q_ref, j, first + i)


SMEM = pl.BlockSpec(memory_space=pltpu.SMEM)
VMEM = pl.BlockSpec(memory_space=pltpu.VMEM)
HBM = pl.BlockSpec(memory_space=pltpu.HBM)


def mask_x(pattern, x):
    return pl.pallas_call(
        mask_x_kernel,
        in_specs=[SMEM, VMEM],
        out_specs=VMEM,
        out_shape=jax.ShapeDtypeStruct((ROWS, COLS), jnp.bfloat16),
        compiler_params=pltpu.CompilerParams(vmem_limit_bytes=8 * 2**20),
        cost_estimate=pl.CostEstimate(flops=ROWS * COLS, bytes_accessed=4 * ROWS * COLS, transcendentals=0),
        name="mask_x",
    )(pattern, x)


def mask_y(where, pattern, pattern_peer, y, y_peer):
    return pl.pallas_call(
        mask_y_kernel,
        in_specs=[SMEM] * 3 + [VMEM] * 2,
        out_specs=VMEM,
        out_shape=jax.ShapeDtypeStruct((ROWS // 2, 2 * COLS), jnp.bfloat16),
        compiler_params=pltpu.CompilerParams(vmem_limit_bytes=8 * 2**20),
        cost_estimate=pl.CostEstimate(flops=ROWS * COLS, bytes_accessed=6 * ROWS * COLS, transcendentals=0),
        name="mask_y",
    )(where, pattern, pattern_peer, y, y_peer)


def after(value, *others):
    return lax.optimization_barrier((value,) + others)[0]


def y_place(where_ref, position):
    yl, xi, yh, z = (where_ref[k] for k in range(4))
    member = position % 4
    offset = jnp.where(member == 0, 0, jnp.where(member == 1, 3, jnp.where(member == 2, 1, 2)))
    gap = (z + offset - xi + 2 * RING) % RING
    y_member = jnp.where(gap == 0, 0, jnp.where(gap == 3, 1, jnp.where(gap == 1, 2, 3)))
    return (yh ^ (position // 4) ^ yl) * 4 + y_member


X_PIECES = ((0, 0, 2), (1, 0, 2), (2, 0, 2), (3, 0, 1), (3, 1, 1), (4, 0, 1), (4, 1, 1), (5, 0, 1), (5, 1, 1), (6, 0, 1), (6, 1, 1))
Y_PIECES = ((0, 0, 2), (1, 0, 2), (2, 0, 2), (3, 0, 1), (3, 1, 1), (4, 0, 2), (5, 0, 2), (6, 0, 2))
EARLY = 7


def early_kernel(*refs):
    nx, ny = len(X_PIECES), len(Y_PIECES)
    x_in, y_in, where_ref = refs[:nx], refs[nx : nx + ny], refs[nx + ny]
    own_ref, far_ref, x_late, y_late = refs[nx + ny + 1 : nx + ny + 5]
    x_buf, y_buf, x_sem, y_sem = refs[nx + ny + 5 :]

    for k in range(max(nx, ny)):
        for pieces, source, buf, sem, half in (
            (X_PIECES, x_in, x_buf, x_sem, ROWS // 2),
            (Y_PIECES, y_in, y_buf, y_sem, ROWS // 4),
        ):
            if k < len(pieces):
                position, start, size = pieces[k]
                target = buf.at[position, pl.ds(start * half, size * half)]
                pltpu.make_async_copy(source[k], target, sem.at[position]).start()

    own_ref[...] = jnp.zeros_like(own_ref)
    far_ref[...] = jnp.zeros_like(far_ref)

    def step(position, carry):
        pltpu.make_async_copy(x_buf.at[position], x_buf.at[position], x_sem.at[position]).wait()
        y_position = y_place(where_ref, position)

        @pl.when(y_position != EARLY)
        def _():
            pltpu.make_async_copy(y_buf.at[y_position], y_buf.at[y_position], y_sem.at[y_position]).wait()
            for out_ref, cols in ((own_ref, slice(0, COLS)), (far_ref, slice(COLS, 2 * COLS))):
                out_ref[...] += jnp.dot(
                    x_buf[position], y_buf[y_position, :, cols], preferred_element_type=jnp.float32
                )

        @pl.when(y_position == EARLY)
        def _():
            x_late[...] = x_buf[position]

        return carry

    lax.fori_loop(0, EARLY, step, 0)
    last = y_place(where_ref, EARLY)

    @pl.when(last != EARLY)
    def _():
        pltpu.make_async_copy(y_buf.at[last], y_buf.at[last], y_sem.at[last]).wait()
        y_late[...] = y_buf[last]


def early_product(x_parts, y_parts, where):
    return pl.pallas_call(
        early_kernel,
        in_specs=[HBM] * (len(X_PIECES) + len(Y_PIECES)) + [SMEM],
        out_specs=[VMEM] * 4,
        out_shape=[
            jax.ShapeDtypeStruct((ROWS, COLS), jnp.float32),
            jax.ShapeDtypeStruct((ROWS, COLS), jnp.float32),
            jax.ShapeDtypeStruct((ROWS, COLS), jnp.bfloat16),
            jax.ShapeDtypeStruct((ROWS // 2, 2 * COLS), jnp.bfloat16),
        ],
        scratch_shapes=[
            pltpu.VMEM((EARLY, ROWS, COLS), jnp.bfloat16),
            pltpu.VMEM((EARLY, ROWS // 2, 2 * COLS), jnp.bfloat16),
            pltpu.SemaphoreType.DMA((EARLY,)),
            pltpu.SemaphoreType.DMA((EARLY,)),
        ],
        compiler_params=pltpu.CompilerParams(vmem_limit_bytes=24 * 2**20),
        cost_estimate=pl.CostEstimate(
            flops=14 * ROWS * COLS * ROWS, bytes_accessed=20 * 2**20, transcendentals=0
        ),
        name="early_product",
    )(*x_parts, *y_parts, where)


def late_kernel(where_ref, x_top, x_bottom, y_top, y_bottom, x_late, y_late, own_ref, far_ref, own_out, far_out):
    last = y_place(where_ref, EARLY)
    quarter = ROWS // 4

    def add(x_far, same_chunk):
        x_last = x_far if same_chunk else x_late
        for sum_ref, out_ref, cols in (
            (own_ref, own_out, slice(0, COLS)),
            (far_ref, far_out, slice(COLS, 2 * COLS)),
        ):
            total = sum_ref[...]
            total += jnp.dot(x_last[:, :quarter], y_top[:, cols], preferred_element_type=jnp.float32)
            total += jnp.dot(x_last[:, quarter:], y_bottom[:, cols], preferred_element_type=jnp.float32)
            if not same_chunk:
                total += jnp.dot(x_far[...], y_late[:, cols], preferred_element_type=jnp.float32)
            out_ref[...] = total

    for upper, x_far in ((True, x_top), (False, x_bottom)):
        for same_chunk in (True, False):
            here = (pl.program_id(0) < 2) == upper
            pl.when(here & ((last == EARLY) == same_chunk))(lambda x=x_far, t=same_chunk: add(x, t))


def late_product(where, x_far, y_far, x_late, y_late, own, far):
    quarter = ROWS // 4
    top = pl.BlockSpec((quarter, COLS), lambda m: (jnp.minimum(m, 1), 0))
    bottom = pl.BlockSpec((quarter, COLS), lambda m: (jnp.maximum(m - 2, 0), 0))
    rows = pl.BlockSpec((quarter, COLS), lambda m: (m, 0))

    def whole(height):
        return pl.BlockSpec((height, 2 * COLS), lambda m: (0, 0))

    return pl.pallas_call(
        late_kernel,
        grid=(4,),
        in_specs=[SMEM, top, bottom, whole(quarter), whole(quarter), rows, whole(2 * quarter), rows, rows],
        out_specs=[rows] * 2,
        out_shape=[jax.ShapeDtypeStruct((ROWS, COLS), jnp.float32)] * 2,
        compiler_params=pltpu.CompilerParams(vmem_limit_bytes=24 * 2**20),
        cost_estimate=pl.CostEstimate(
            flops=4 * ROWS * COLS * ROWS, bytes_accessed=12 * 2**20, transcendentals=0
        ),
        name="late_product",
    )(where, *x_far, *y_far, x_late, y_late, own, far)


def finish_kernel(where_ref, pattern_ref, index_ref, energy_ref, xm_ref, own_ref, peer_ref, sign_ref, payload_ref, dens):
    yl, xi, yh, z, core = (where_ref[k] for k in range(5))
    block_row = (yl * 4 + xi) * RB
    block_col = ((yh * 4 + z) * 2 + core) * QB
    same = lax.broadcasted_iota(jnp.int32, (BS, BS), 0) == lax.broadcasted_iota(jnp.int32, (BS, BS), 1)
    half_eye = jnp.where(same, 0.5, 0.0).astype(jnp.float32)

    def finish(i, carry):
        rows = pl.ds(pl.multiple_of(i * BS, BS), BS)
        for j in range(QB):
            cols = slice(j * BS, (j + 1) * BS)
            kept = jnp.where(pattern_ref[j, i] > 0, 0.5, 0.0)
            product = own_ref[rows, cols] + peer_ref[rows, cols]
            xnew = 1.5 * xm_ref[rows, cols].astype(jnp.float32) - kept * product
            sign_ref[rows, cols] = xnew.astype(jnp.bfloat16)
            on_diagonal = jnp.where(block_row + i == block_col + j, 1.0, 0.0)
            dens[i * QB + j] = (on_diagonal * half_eye - 0.5 * xnew).astype(jnp.bfloat16)
        return carry

    lax.fori_loop(0, RB, finish, 0)
    dens[BLOCKS] = jnp.zeros((BS, BS), jnp.bfloat16)

    line = lax.broadcasted_iota(jnp.int32, (TAIL, BS), 0)

    def copy(owner, carry):
        energies = jnp.zeros((TAIL, BS), jnp.float32)
        for k in range(CAP):
            block = index_ref[owner * CAP + k]
            payload_ref[owner, k * BS : (k + 1) * BS, :] = dens[block]
            energies = jnp.where(line == k, energy_ref[block // QB], energies)
        payload_ref[owner, CAP * BS :, :] = energies.astype(jnp.bfloat16)
        return carry

    lax.fori_loop(0, payload_ref.shape[0], copy, 0, unroll=4)


def finish_and_payload(where, pattern, index, energy, xm, own, peer):
    owners = index.shape[0] // CAP
    packet = (owners, CAP * BS + TAIL, BS)
    return pl.pallas_call(
        finish_kernel,
        in_specs=[SMEM] * 3 + [VMEM] * 4,
        out_specs=[VMEM, VMEM],
        out_shape=[
            jax.ShapeDtypeStruct((ROWS, COLS), jnp.bfloat16),
            jax.ShapeDtypeStruct(packet, jnp.bfloat16),
        ],
        scratch_shapes=[
            pltpu.VMEM((BLOCKS + 1, BS, BS), jnp.bfloat16),
        ],
        compiler_params=pltpu.CompilerParams(vmem_limit_bytes=18 * 2**20),
        cost_estimate=pl.CostEstimate(flops=4 * ROWS * COLS, bytes_accessed=15 * 2**20, transcendentals=0),
        name="finish_payload",
    )(where, pattern, index, energy, xm, own, peer)


FCH = 16


def force_kernel(d_ref, h_ref, s_ref, out_ref):
    same = lax.broadcasted_iota(jnp.int32, (BS, BS), 0) == lax.broadcasted_iota(jnp.int32, (BS, BS), 1)
    ones = jnp.ones((BS, BS), jnp.bfloat16)
    for source in range(FCH):
        energies = d_ref[source, CAP * BS :, :].astype(jnp.float32)
        for k in range(CAP):
            slot = source * CAP + k
            spread = jnp.where(same, energies[k : k + 1, :], 0.0).astype(jnp.bfloat16)
            energy = jnp.dot(spread, ones, preferred_element_type=jnp.float32)
            term = d_ref[source, k * BS : (k + 1) * BS, :].astype(jnp.float32) * (
                h_ref[slot].astype(jnp.float32) - energy * s_ref[slot].astype(jnp.float32)
            )
            out_ref[slot : slot + 1, :] = jnp.sum(term, axis=0, keepdims=True)


def force_sums(packets, force_h, force_s):
    slots = force_h.shape[0]
    block = pl.BlockSpec((FCH * CAP, BS, BS), lambda i: (i, 0, 0))
    partial = pl.pallas_call(
        force_kernel,
        grid=(slots // (FCH * CAP),),
        in_specs=[pl.BlockSpec((FCH, CAP * BS + TAIL, BS), lambda i: (i, 0, 0)), block, block],
        out_specs=pl.BlockSpec((FCH * CAP, BS), lambda i: (i, 0)),
        out_shape=jax.ShapeDtypeStruct((slots, BS), jnp.float32),
        compiler_params=pltpu.CompilerParams(vmem_limit_bytes=12 * 2**20),
        cost_estimate=pl.CostEstimate(
            flops=6 * slots * BS * BS, bytes_accessed=6 * slots * BS * BS, transcendentals=0
        ),
        name="force_sums",
    )(packets, force_h, force_s)
    return jnp.sum(partial, axis=1)


def exchange(payload):
    return lax.all_to_all(payload, AXES, split_axis=0, concat_axis=0, tiled=True)


def shards(x, y, pattern_x, pattern_y, pattern_product, orbital_energy, pair_dest, pair_block, force_h, force_s):
    dest, wanted = pair_dest[0, :, 0], pair_block[0]
    slots = force_h.shape[0]
    entries = dest.shape[0]
    order = jnp.arange(entries, dtype=jnp.int32)
    earlier = (dest[:, None] == dest[None, :]) & (order[None, :] < order[:, None])
    rank = jnp.sum(earlier.astype(jnp.int32), axis=1)
    slot = dest * CAP + rank
    named = slot[None, :] == jnp.arange(slots, dtype=jnp.int32)[:, None]
    index = jnp.sum(jnp.where(named, wanted[None, :] - BLOCKS, 0), axis=1) + BLOCKS
    energy = jnp.pad(orbital_energy.astype(jnp.float32).reshape(RB, 1, BS), ((0, 1), (0, 0), (0, 0)))

    where = jnp.stack([lax.axis_index(axis) for axis in AXES]).astype(jnp.int32)
    half, quarter = ROWS // 2, ROWS // 4
    y_peer = lax.ppermute(y, "c", SWAP)
    pattern_peer = lax.ppermute(pattern_y.T, "c", SWAP)
    xm = mask_x(pattern_x.T, x)
    ym = mask_y(where, pattern_y.T, pattern_peer, y, y_peer)

    xb_top = lax.ppermute(xm[:half], "yh", SWAP)
    xa_below = lax.ppermute(xm, "z", UP)
    xa_above = lax.ppermute(xm, "z", DOWN)
    ya_below = lax.ppermute(ym, "x", UP)
    ya_above = lax.ppermute(ym, "x", DOWN)
    yb = lax.ppermute(after(ym, xb_top), "yl", SWAP)
    xb_bottom = lax.ppermute(after(xm[half:], yb), "yh", SWAP)

    xa_far = [lax.ppermute(xa_below[:half], "z", UP), lax.ppermute(xa_above[half:], "z", DOWN)]
    ya_far = [lax.ppermute(ya_below[:quarter], "x", UP), lax.ppermute(ya_above[quarter:], "x", DOWN)]

    xb_top_z = after(xb_top, *xa_far)
    xbt_below, xbt_above = lax.ppermute(xb_top_z, "z", UP), lax.ppermute(xb_top_z, "z", DOWN)
    yb_x = after(yb, *ya_far)
    yb_below, yb_above = lax.ppermute(yb_x, "x", UP), lax.ppermute(yb_x, "x", DOWN)
    xb_bottom_z = after(xb_bottom, xbt_below, xbt_above)
    xbb_below, xbb_above = lax.ppermute(xb_bottom_z, "z", UP), lax.ppermute(xb_bottom_z, "z", DOWN)

    xb_far = [
        lax.ppermute(after(xbt_below, xbb_below), "z", UP),
        lax.ppermute(xbb_above, "z", DOWN),
    ]
    yb_far = [lax.ppermute(yb_below[:quarter], "x", UP), lax.ppermute(yb_above[quarter:], "x", DOWN)]

    x_parts = [xm, xa_below, xa_above, *xa_far, xb_top, xb_bottom, xbt_below, xbb_below, xbt_above, xbb_above]
    y_parts = [ym, ya_below, ya_above, *ya_far, yb, yb_below, yb_above]
    own, far, x_late, y_late = early_product(x_parts, y_parts, where)
    own, far = late_product(where, xb_far, yb_far, x_late, y_late, own, far)
    peer = lax.ppermute(far, "c", SWAP)
    sign_next, payload = finish_and_payload(where, pattern_product.T, index, energy, xm, own, peer)
    received = exchange(payload)
    return sign_next, force_sums(received, force_h, force_s)


def solution(mesh):
    fine = Mesh(mesh.devices.reshape(2, 4, 2, 4, 2), AXES)
    row, col = ("yl", "x"), ("yh", "z", "c")
    in_specs = (
        P(row, col),
        P(row, col),
        P(row, col),
        P(row, col),
        P(row, col),
        P(row),
        P(AXES, None, None),
        P(AXES, None),
        P(AXES, None, None),
        P(AXES, None, None),
    )
    out_specs = (P(row, col), P(AXES))
    return jax.shard_map(shards, mesh=fine, in_specs=in_specs, out_specs=out_specs, check_vma=False)
```

```python
import jax
import jax.numpy as jnp
from jax import lax
from jax.experimental import pallas as pl
from jax.experimental.pallas import tpu as pltpu
from jax.sharding import Mesh, PartitionSpec as P

BS = 128
QB = 4
CAP = 2
RB = 8
BLOCKS = RB * QB
TAIL = 8
ROWS = RB * BS
COLS = QB * BS
RING = 4
AXES = ("yl", "x", "yh", "z", "c")
SWAP = [(0, 1), (1, 0)]
UP = [(i, (i + 1) % RING) for i in range(RING)]
DOWN = [(i, (i - 1) % RING) for i in range(RING)]


def keep_block(pattern_ref, j, i):
    return (pattern_ref[j, i] > 0).astype(jnp.float32).astype(jnp.bfloat16)


def mask_x_kernel(p_ref, x_ref, o_ref):
    for i in range(RB):
        for j in range(QB):
            rows, cols = slice(i * BS, (i + 1) * BS), slice(j * BS, (j + 1) * BS)
            o_ref[rows, cols] = x_ref[rows, cols] * keep_block(p_ref, j, i)


def mask_y_kernel(where_ref, p_ref, q_ref, y_ref, z_ref, o_ref):
    first = where_ref[4] * (RB // 2)
    for i in range(RB // 2):
        rows = slice(i * BS, (i + 1) * BS)
        own_rows = pl.ds(pl.multiple_of((first + i) * BS, BS), BS)
        for j in range(QB):
            cols = slice(j * BS, (j + 1) * BS)
            far_cols = slice(COLS + j * BS, COLS + (j + 1) * BS)
            o_ref[rows, cols] = y_ref[own_rows, cols] * keep_block(p_ref, j, first + i)
            o_ref[rows, far_cols] = z_ref[own_rows, cols] * keep_block(q_ref, j, first + i)


SMEM = pl.BlockSpec(memory_space=pltpu.SMEM)
VMEM = pl.BlockSpec(memory_space=pltpu.VMEM)
HBM = pl.BlockSpec(memory_space=pltpu.HBM)


def mask_x(pattern, x):
    return pl.pallas_call(
        mask_x_kernel,
        in_specs=[SMEM, VMEM],
        out_specs=VMEM,
        out_shape=jax.ShapeDtypeStruct((ROWS, COLS), jnp.bfloat16),
        compiler_params=pltpu.CompilerParams(vmem_limit_bytes=8 * 2**20),
        cost_estimate=pl.CostEstimate(flops=ROWS * COLS, bytes_accessed=4 * ROWS * COLS, transcendentals=0),
        name="mask_x",
    )(pattern, x)


def mask_y(where, pattern, pattern_peer, y, y_peer):
    return pl.pallas_call(
        mask_y_kernel,
        in_specs=[SMEM] * 3 + [VMEM] * 2,
        out_specs=VMEM,
        out_shape=jax.ShapeDtypeStruct((ROWS // 2, 2 * COLS), jnp.bfloat16),
        compiler_params=pltpu.CompilerParams(vmem_limit_bytes=8 * 2**20),
        cost_estimate=pl.CostEstimate(flops=ROWS * COLS, bytes_accessed=6 * ROWS * COLS, transcendentals=0),
        name="mask_y",
    )(where, pattern, pattern_peer, y, y_peer)


def after(value, *others):
    return lax.optimization_barrier((value,) + others)[0]


def y_place(where_ref, position):
    yl, xi, yh, z = (where_ref[k] for k in range(4))
    member = position % 4
    offset = jnp.where(member == 0, 0, jnp.where(member == 1, 3, jnp.where(member == 2, 1, 2)))
    gap = (z + offset - xi + 2 * RING) % RING
    y_member = jnp.where(gap == 0, 0, jnp.where(gap == 3, 1, jnp.where(gap == 1, 2, 3)))
    return (yh ^ (position // 4) ^ yl) * 4 + y_member


X_PIECES = ((0, 0, 2), (1, 0, 2), (2, 0, 2), (3, 0, 1), (3, 1, 1), (4, 0, 1), (4, 1, 1), (5, 0, 1), (5, 1, 1), (6, 0, 1), (6, 1, 1))
Y_PIECES = ((0, 0, 2), (1, 0, 2), (2, 0, 2), (3, 0, 1), (3, 1, 1), (4, 0, 2), (5, 0, 2), (6, 0, 2))
EARLY = 7


def early_kernel(*refs):
    nx, ny = len(X_PIECES), len(Y_PIECES)
    x_in, y_in, where_ref = refs[:nx], refs[nx : nx + ny], refs[nx + ny]
    own_ref, far_ref, x_late, y_late = refs[nx + ny + 1 : nx + ny + 5]
    x_buf, y_buf, x_sem, y_sem = refs[nx + ny + 5 :]

    for k in range(max(nx, ny)):
        for pieces, source, buf, sem, half in (
            (X_PIECES, x_in, x_buf, x_sem, ROWS // 2),
            (Y_PIECES, y_in, y_buf, y_sem, ROWS // 4),
        ):
            if k < len(pieces):
                position, start, size = pieces[k]
                target = buf.at[position, pl.ds(start * half, size * half)]
                pltpu.make_async_copy(source[k], target, sem.at[position]).start()

    own_ref[...] = jnp.zeros_like(own_ref)
    far_ref[...] = jnp.zeros_like(far_ref)

    def step(position, carry):
        pltpu.make_async_copy(x_buf.at[position], x_buf.at[position], x_sem.at[position]).wait()
        y_position = y_place(where_ref, position)

        @pl.when(y_position != EARLY)
        def _():
            pltpu.make_async_copy(y_buf.at[y_position], y_buf.at[y_position], y_sem.at[y_position]).wait()
            for out_ref, cols in ((own_ref, slice(0, COLS)), (far_ref, slice(COLS, 2 * COLS))):
                out_ref[...] += jnp.dot(
                    x_buf[position], y_buf[y_position, :, cols], preferred_element_type=jnp.float32
                )

        @pl.when(y_position == EARLY)
        def _():
            x_late[...] = x_buf[position]

        return carry

    lax.fori_loop(0, EARLY, step, 0)
    last = y_place(where_ref, EARLY)

    @pl.when(last != EARLY)
    def _():
        pltpu.make_async_copy(y_buf.at[last], y_buf.at[last], y_sem.at[last]).wait()
        y_late[...] = y_buf[last]


def early_product(x_parts, y_parts, where):
    return pl.pallas_call(
        early_kernel,
        in_specs=[HBM] * (len(X_PIECES) + len(Y_PIECES)) + [SMEM],
        out_specs=[VMEM] * 4,
        out_shape=[
            jax.ShapeDtypeStruct((ROWS, COLS), jnp.float32),
            jax.ShapeDtypeStruct((ROWS, COLS), jnp.float32),
            jax.ShapeDtypeStruct((ROWS, COLS), jnp.bfloat16),
            jax.ShapeDtypeStruct((ROWS // 2, 2 * COLS), jnp.bfloat16),
        ],
        scratch_shapes=[
            pltpu.VMEM((EARLY, ROWS, COLS), jnp.bfloat16),
            pltpu.VMEM((EARLY, ROWS // 2, 2 * COLS), jnp.bfloat16),
            pltpu.SemaphoreType.DMA((EARLY,)),
            pltpu.SemaphoreType.DMA((EARLY,)),
        ],
        compiler_params=pltpu.CompilerParams(vmem_limit_bytes=24 * 2**20),
        cost_estimate=pl.CostEstimate(
            flops=14 * ROWS * COLS * ROWS, bytes_accessed=20 * 2**20, transcendentals=0
        ),
        name="early_product",
    )(*x_parts, *y_parts, where)


def late_kernel(where_ref, x_top, x_bottom, y_top, y_bottom, x_late, y_late, sum_ref, out_ref):
    last = y_place(where_ref, EARLY)
    quarter = ROWS // 4

    def add(x_far, same_chunk):
        x_last = x_far if same_chunk else x_late
        total = sum_ref[...]
        total += jnp.dot(x_last[:, :quarter], y_top[...], preferred_element_type=jnp.float32)
        total += jnp.dot(x_last[:, quarter:], y_bottom[...], preferred_element_type=jnp.float32)
        if not same_chunk:
            total += jnp.dot(x_far[...], y_late[...], preferred_element_type=jnp.float32)
        out_ref[...] = total

    for upper, x_far in ((True, x_top), (False, x_bottom)):
        for same_chunk in (True, False):
            here = (pl.program_id(0) < 1) == upper
            pl.when(here & ((last == EARLY) == same_chunk))(lambda x=x_far, t=same_chunk: add(x, t))


def late_product(side, where, x_far, y_far, x_late, y_late, total):
    half, quarter = ROWS // 2, ROWS // 4
    rows = pl.BlockSpec((half, COLS), lambda m: (m, 0))
    whole = pl.BlockSpec((half, COLS), lambda m: (0, 0))

    def columns(height):
        return pl.BlockSpec((height, COLS), lambda m: (0, side))

    return pl.pallas_call(
        late_kernel,
        grid=(2,),
        in_specs=[SMEM, whole, whole, columns(quarter), columns(quarter), rows, columns(half), rows],
        out_specs=rows,
        out_shape=jax.ShapeDtypeStruct((ROWS, COLS), jnp.float32),
        compiler_params=pltpu.CompilerParams(vmem_limit_bytes=16 * 2**20),
        cost_estimate=pl.CostEstimate(
            flops=2 * ROWS * COLS * ROWS, bytes_accessed=8 * 2**20, transcendentals=0
        ),
        name="late_product",
    )(where, *x_far, *y_far, x_late, y_late, total)


def finish_kernel(where_ref, pattern_ref, index_ref, energy_ref, xm_ref, own_ref, peer_ref, sign_out, payload_ref, dens, sign_ref, sign_sem):
    yl, xi, yh, z, core = (where_ref[k] for k in range(5))
    block_row = (yl * 4 + xi) * RB
    block_col = ((yh * 4 + z) * 2 + core) * QB
    same = lax.broadcasted_iota(jnp.int32, (BS, BS), 0) == lax.broadcasted_iota(jnp.int32, (BS, BS), 1)
    half_eye = jnp.where(same, 0.5, 0.0).astype(jnp.float32)

    def finish(i, carry):
        rows = pl.ds(pl.multiple_of(i * BS, BS), BS)
        for j in range(QB):
            cols = slice(j * BS, (j + 1) * BS)
            kept = jnp.where(pattern_ref[j, i] > 0, 0.5, 0.0)
            product = own_ref[rows, cols] + peer_ref[rows, cols]
            xnew = 1.5 * xm_ref[rows, cols].astype(jnp.float32) - kept * product
            sign_ref[rows, cols] = xnew.astype(jnp.bfloat16)
            on_diagonal = jnp.where(block_row + i == block_col + j, 1.0, 0.0)
            dens[i * QB + j] = (on_diagonal * half_eye - 0.5 * xnew).astype(jnp.bfloat16)
        return carry

    lax.fori_loop(0, RB, finish, 0)
    sign_copy = pltpu.make_async_copy(sign_ref, sign_out, sign_sem)
    sign_copy.start()
    dens[BLOCKS] = jnp.zeros((BS, BS), jnp.bfloat16)

    line = lax.broadcasted_iota(jnp.int32, (TAIL, BS), 0)

    def copy(owner, carry):
        energies = jnp.zeros((TAIL, BS), jnp.float32)
        for k in range(CAP):
            block = index_ref[owner * CAP + k]
            payload_ref[owner, k * BS : (k + 1) * BS, :] = dens[block]
            energies = jnp.where(line == k, energy_ref[block // QB], energies)
        payload_ref[owner, CAP * BS :, :] = energies.astype(jnp.bfloat16)
        return carry

    lax.fori_loop(0, payload_ref.shape[0], copy, 0, unroll=4)
    sign_copy.wait()


def finish_and_payload(where, pattern, index, energy, xm, own, peer):
    owners = index.shape[0] // CAP
    packet = (owners, CAP * BS + TAIL, BS)
    return pl.pallas_call(
        finish_kernel,
        in_specs=[SMEM] * 3 + [VMEM] * 4,
        out_specs=[HBM, VMEM],
        out_shape=[
            jax.ShapeDtypeStruct((ROWS, COLS), jnp.bfloat16),
            jax.ShapeDtypeStruct(packet, jnp.bfloat16),
        ],
        scratch_shapes=[
            pltpu.VMEM((BLOCKS + 1, BS, BS), jnp.bfloat16),
            pltpu.VMEM((ROWS, COLS), jnp.bfloat16),
            pltpu.SemaphoreType.DMA,
        ],
        compiler_params=pltpu.CompilerParams(vmem_limit_bytes=18 * 2**20),
        cost_estimate=pl.CostEstimate(flops=4 * ROWS * COLS, bytes_accessed=15 * 2**20, transcendentals=0),
        name="finish_payload",
    )(where, pattern, index, energy, xm, own, peer)


FCH = 16


def force_kernel(d_ref, h_ref, s_ref, out_ref, part_ref):
    same = lax.broadcasted_iota(jnp.int32, (BS, BS), 0) == lax.broadcasted_iota(jnp.int32, (BS, BS), 1)
    ones = jnp.ones((BS, BS), jnp.bfloat16)

    def group(i, carry):
        for j in range(FCH):
            source = i * FCH + j
            energies = d_ref[source, CAP * BS :, :].astype(jnp.float32)
            for k in range(CAP):
                slot = source * CAP + k
                spread = jnp.where(same, energies[k : k + 1, :], 0.0).astype(jnp.bfloat16)
                energy = jnp.dot(spread, ones, preferred_element_type=jnp.float32)
                term = d_ref[source, k * BS : (k + 1) * BS, :].astype(jnp.float32) * (
                    h_ref[slot].astype(jnp.float32) - energy * s_ref[slot].astype(jnp.float32)
                )
                row = j * CAP + k
                part_ref[i, row : row + 1, :] = jnp.sum(term, axis=0, keepdims=True)
        return carry

    lax.fori_loop(0, part_ref.shape[0], group, 0)
    parts = part_ref[...].reshape(out_ref.shape[0], BS)
    out_ref[...] = lax.dot_general(
        jnp.ones((8, BS), jnp.float32),
        parts,
        (((1,), (1,)), ((), ())),
        precision=lax.Precision.HIGHEST,
        preferred_element_type=jnp.float32,
    )[0]


def force_sums(packets, force_h, force_s):
    slots = force_h.shape[0]
    return pl.pallas_call(
        force_kernel,
        in_specs=[VMEM] * 3,
        out_specs=VMEM,
        out_shape=jax.ShapeDtypeStruct((slots,), jnp.float32),
        scratch_shapes=[pltpu.VMEM((slots // (FCH * CAP), FCH * CAP, BS), jnp.float32)],
        compiler_params=pltpu.CompilerParams(vmem_limit_bytes=12 * 2**20),
        cost_estimate=pl.CostEstimate(
            flops=6 * slots * BS * BS, bytes_accessed=6 * slots * BS * BS, transcendentals=0
        ),
        name="force_sums",
    )(packets, force_h, force_s)


def exchange(payload):
    return lax.all_to_all(payload, AXES, split_axis=0, concat_axis=0, tiled=True)


def shards(x, y, pattern_x, pattern_y, pattern_product, orbital_energy, pair_dest, pair_block, force_h, force_s):
    dest, wanted = pair_dest[0, :, 0], pair_block[0]
    slots = force_h.shape[0]
    entries = dest.shape[0]
    order = jnp.arange(entries, dtype=jnp.int32)
    earlier = (dest[:, None] == dest[None, :]) & (order[None, :] < order[:, None])
    rank = jnp.sum(earlier.astype(jnp.int32), axis=1)
    slot = dest * CAP + rank
    named = slot[None, :] == jnp.arange(slots, dtype=jnp.int32)[:, None]
    index = jnp.sum(jnp.where(named, wanted[None, :] - BLOCKS, 0), axis=1) + BLOCKS
    energy = jnp.pad(orbital_energy.astype(jnp.float32).reshape(RB, 1, BS), ((0, 1), (0, 0), (0, 0)))

    where = jnp.stack([lax.axis_index(axis) for axis in AXES]).astype(jnp.int32)
    half, quarter = ROWS // 2, ROWS // 4
    y_peer = lax.ppermute(y, "c", SWAP)
    pattern_peer = lax.ppermute(pattern_y.T, "c", SWAP)
    xm = mask_x(pattern_x.T, x)
    ym = mask_y(where, pattern_y.T, pattern_peer, y, y_peer)

    xb_top = lax.ppermute(xm[:half], "yh", SWAP)
    xa_below = lax.ppermute(xm, "z", UP)
    xa_above = lax.ppermute(xm, "z", DOWN)
    ya_below = lax.ppermute(ym, "x", UP)
    ya_above = lax.ppermute(ym, "x", DOWN)
    yb = lax.ppermute(after(ym, xb_top), "yl", SWAP)
    xb_bottom = lax.ppermute(after(xm[half:], yb), "yh", SWAP)

    xa_far = [lax.ppermute(xa_below[:half], "z", UP), lax.ppermute(xa_above[half:], "z", DOWN)]
    ya_far = [lax.ppermute(ya_below[:quarter], "x", UP), lax.ppermute(ya_above[quarter:], "x", DOWN)]

    xb_top_z = after(xb_top, *xa_far)
    xbt_below, xbt_above = lax.ppermute(xb_top_z, "z", UP), lax.ppermute(xb_top_z, "z", DOWN)
    yb_x = after(yb, *ya_far)
    yb_below, yb_above = lax.ppermute(yb_x, "x", UP), lax.ppermute(yb_x, "x", DOWN)
    xb_bottom_z = after(xb_bottom, xbt_below, xbt_above)
    xbb_below, xbb_above = lax.ppermute(xb_bottom_z, "z", UP), lax.ppermute(xb_bottom_z, "z", DOWN)

    xb_far = [
        lax.ppermute(after(xbt_below, xbb_below), "z", UP),
        lax.ppermute(xbb_above, "z", DOWN),
    ]
    yb_far = [lax.ppermute(yb_below[:quarter], "x", UP), lax.ppermute(yb_above[quarter:], "x", DOWN)]

    x_parts = [xm, xa_below, xa_above, *xa_far, xb_top, xb_bottom, xbt_below, xbb_below, xbt_above, xbb_above]
    y_parts = [ym, ya_below, ya_above, *ya_far, yb, yb_below, yb_above]
    own, far, x_late, y_late = early_product(x_parts, y_parts, where)
    far = late_product(1, where, xb_far, yb_far, x_late, y_late, far)
    peer = lax.ppermute(far, "c", SWAP)
    own = late_product(0, where, xb_far, yb_far, x_late, y_late, after(own, far))
    sign_next, payload = finish_and_payload(where, pattern_product.T, index, energy, xm, own, peer)
    received = exchange(payload)
    return sign_next, force_sums(received, force_h, force_s)


def solution(mesh):
    fine = Mesh(mesh.devices.reshape(2, 4, 2, 4, 2), AXES)
    row, col = ("yl", "x"), ("yh", "z", "c")
    in_specs = (
        P(row, col),
        P(row, col),
        P(row, col),
        P(row, col),
        P(row, col),
        P(row),
        P(AXES, None, None),
        P(AXES, None),
        P(AXES, None, None),
        P(AXES, None, None),
    )
    out_specs = (P(row, col), P(AXES))
    return jax.shard_map(shards, mesh=fine, in_specs=in_specs, out_specs=out_specs, check_vma=False)
```

```python
import jax
import jax.numpy as jnp
from jax import lax
from jax.experimental import pallas as pl
from jax.experimental.pallas import tpu as pltpu
from jax.sharding import Mesh, PartitionSpec as P

BS = 128
QB = 4
CAP = 2
RB = 8
BLOCKS = RB * QB
TAIL = 8
ROWS = RB * BS
COLS = QB * BS
RING = 4
AXES = ("yl", "x", "yh", "z", "c")
SWAP = [(0, 1), (1, 0)]
UP = [(i, (i + 1) % RING) for i in range(RING)]
DOWN = [(i, (i - 1) % RING) for i in range(RING)]


def keep_block(pattern_ref, j, i):
    return (pattern_ref[j, i] > 0).astype(jnp.float32).astype(jnp.bfloat16)


def mask_x_kernel(p_ref, x_ref, o_ref):
    for i in range(RB):
        for j in range(QB):
            rows, cols = slice(i * BS, (i + 1) * BS), slice(j * BS, (j + 1) * BS)
            o_ref[rows, cols] = x_ref[rows, cols] * keep_block(p_ref, j, i)


def mask_y_kernel(where_ref, p_ref, q_ref, y_ref, z_ref, o_ref):
    first = where_ref[4] * (RB // 2)
    for i in range(RB // 2):
        rows = slice(i * BS, (i + 1) * BS)
        own_rows = pl.ds(pl.multiple_of((first + i) * BS, BS), BS)
        for j in range(QB):
            cols = slice(j * BS, (j + 1) * BS)
            far_cols = slice(COLS + j * BS, COLS + (j + 1) * BS)
            o_ref[rows, cols] = y_ref[own_rows, cols] * keep_block(p_ref, j, first + i)
            o_ref[rows, far_cols] = z_ref[own_rows, cols] * keep_block(q_ref, j, first + i)


SMEM = pl.BlockSpec(memory_space=pltpu.SMEM)
VMEM = pl.BlockSpec(memory_space=pltpu.VMEM)
HBM = pl.BlockSpec(memory_space=pltpu.HBM)


def mask_x(pattern, x):
    return pl.pallas_call(
        mask_x_kernel,
        in_specs=[SMEM, VMEM],
        out_specs=VMEM,
        out_shape=jax.ShapeDtypeStruct((ROWS, COLS), jnp.bfloat16),
        compiler_params=pltpu.CompilerParams(vmem_limit_bytes=8 * 2**20),
        cost_estimate=pl.CostEstimate(flops=ROWS * COLS, bytes_accessed=4 * ROWS * COLS, transcendentals=0),
        name="mask_x",
    )(pattern, x)


def mask_y(where, pattern, pattern_peer, y, y_peer):
    return pl.pallas_call(
        mask_y_kernel,
        in_specs=[SMEM] * 3 + [VMEM] * 2,
        out_specs=VMEM,
        out_shape=jax.ShapeDtypeStruct((ROWS // 2, 2 * COLS), jnp.bfloat16),
        compiler_params=pltpu.CompilerParams(vmem_limit_bytes=8 * 2**20),
        cost_estimate=pl.CostEstimate(flops=ROWS * COLS, bytes_accessed=6 * ROWS * COLS, transcendentals=0),
        name="mask_y",
    )(where, pattern, pattern_peer, y, y_peer)


def after(value, *others):
    return lax.optimization_barrier((value,) + others)[0]


def y_place(where_ref, position):
    yl, xi, yh, z = (where_ref[k] for k in range(4))
    member = position % 4
    offset = jnp.where(member == 0, 0, jnp.where(member == 1, 3, jnp.where(member == 2, 1, 2)))
    gap = (z + offset - xi + 2 * RING) % RING
    y_member = jnp.where(gap == 0, 0, jnp.where(gap == 3, 1, jnp.where(gap == 1, 2, 3)))
    return (yh ^ (position // 4) ^ yl) * 4 + y_member


X_PIECES = ((0, 0, 2), (1, 0, 2), (2, 0, 2), (3, 0, 1), (3, 1, 1), (4, 0, 1), (4, 1, 1), (5, 0, 1), (5, 1, 1), (6, 0, 1), (6, 1, 1))
Y_PIECES = ((0, 0, 2), (1, 0, 2), (2, 0, 2), (3, 0, 1), (3, 1, 1), (4, 0, 2), (5, 0, 2), (6, 0, 2))
EARLY = 7


def early_kernel(*refs):
    nx, ny = len(X_PIECES), len(Y_PIECES)
    x_in, y_in, where_ref = refs[:nx], refs[nx : nx + ny], refs[nx + ny]
    own_ref, far_ref, x_late, y_late = refs[nx + ny + 1 : nx + ny + 5]
    x_buf, y_buf, x_sem, y_sem = refs[nx + ny + 5 :]

    for k in range(max(nx, ny)):
        for pieces, source, buf, sem, half in (
            (X_PIECES, x_in, x_buf, x_sem, ROWS // 2),
            (Y_PIECES, y_in, y_buf, y_sem, ROWS // 4),
        ):
            if k < len(pieces):
                position, start, size = pieces[k]
                target = buf.at[position, pl.ds(start * half, size * half)]
                pltpu.make_async_copy(source[k], target, sem.at[position]).start()

    own_ref[...] = jnp.zeros_like(own_ref)
    far_ref[...] = jnp.zeros_like(far_ref)

    def step(position, carry):
        pltpu.make_async_copy(x_buf.at[position], x_buf.at[position], x_sem.at[position]).wait()
        y_position = y_place(where_ref, position)

        @pl.when(y_position != EARLY)
        def _():
            pltpu.make_async_copy(y_buf.at[y_position], y_buf.at[y_position], y_sem.at[y_position]).wait()
            for out_ref, cols in ((own_ref, slice(0, COLS)), (far_ref, slice(COLS, 2 * COLS))):
                out_ref[...] += jnp.dot(
                    x_buf[position], y_buf[y_position, :, cols], preferred_element_type=jnp.float32
                )

        @pl.when(y_position == EARLY)
        def _():
            x_late[...] = x_buf[position]

        return carry

    lax.fori_loop(0, EARLY, step, 0)
    last = y_place(where_ref, EARLY)

    @pl.when(last != EARLY)
    def _():
        pltpu.make_async_copy(y_buf.at[last], y_buf.at[last], y_sem.at[last]).wait()
        y_late[...] = y_buf[last]


def early_product(x_parts, y_parts, where):
    return pl.pallas_call(
        early_kernel,
        in_specs=[HBM] * (len(X_PIECES) + len(Y_PIECES)) + [SMEM],
        out_specs=[VMEM] * 4,
        out_shape=[
            jax.ShapeDtypeStruct((ROWS, COLS), jnp.float32),
            jax.ShapeDtypeStruct((ROWS, COLS), jnp.float32),
            jax.ShapeDtypeStruct((ROWS, COLS), jnp.bfloat16),
            jax.ShapeDtypeStruct((ROWS // 2, 2 * COLS), jnp.bfloat16),
        ],
        scratch_shapes=[
            pltpu.VMEM((EARLY, ROWS, COLS), jnp.bfloat16),
            pltpu.VMEM((EARLY, ROWS // 2, 2 * COLS), jnp.bfloat16),
            pltpu.SemaphoreType.DMA((EARLY,)),
            pltpu.SemaphoreType.DMA((EARLY,)),
        ],
        compiler_params=pltpu.CompilerParams(vmem_limit_bytes=24 * 2**20),
        cost_estimate=pl.CostEstimate(
            flops=14 * ROWS * COLS * ROWS, bytes_accessed=20 * 2**20, transcendentals=0
        ),
        name="early_product",
    )(*x_parts, *y_parts, where)


def late_kernel(where_ref, x_top, x_bottom, y_top, y_bottom, x_late, y_late, sum_ref, out_ref):
    last = y_place(where_ref, EARLY)
    quarter = ROWS // 4

    def add(x_far, same_chunk):
        x_last = x_far if same_chunk else x_late
        total = sum_ref[...]
        total += jnp.dot(x_last[:, :quarter], y_top[...], preferred_element_type=jnp.float32)
        total += jnp.dot(x_last[:, quarter:], y_bottom[...], preferred_element_type=jnp.float32)
        if not same_chunk:
            total += jnp.dot(x_far[...], y_late[...], preferred_element_type=jnp.float32)
        out_ref[...] = total

    for upper, x_far in ((True, x_top), (False, x_bottom)):
        for same_chunk in (True, False):
            here = (pl.program_id(0) < 1) == upper
            pl.when(here & ((last == EARLY) == same_chunk))(lambda x=x_far, t=same_chunk: add(x, t))


def late_product(side, where, x_far, y_far, x_late, y_late, total):
    half, quarter = ROWS // 2, ROWS // 4
    rows = pl.BlockSpec((half, COLS), lambda m: (m, 0))
    whole = pl.BlockSpec((half, COLS), lambda m: (0, 0))

    def columns(height):
        return pl.BlockSpec((height, COLS), lambda m: (0, side))

    return pl.pallas_call(
        late_kernel,
        grid=(2,),
        in_specs=[SMEM, whole, whole, columns(quarter), columns(quarter), rows, columns(half), rows],
        out_specs=rows,
        out_shape=jax.ShapeDtypeStruct((ROWS, COLS), jnp.float32),
        compiler_params=pltpu.CompilerParams(vmem_limit_bytes=16 * 2**20),
        cost_estimate=pl.CostEstimate(
            flops=2 * ROWS * COLS * ROWS, bytes_accessed=8 * 2**20, transcendentals=0
        ),
        name="late_product",
    )(where, *x_far, *y_far, x_late, y_late, total)


def finish_kernel(where_ref, pattern_ref, index_ref, energy_ref, xm_ref, own_ref, peer_ref, sign_out, payload_ref, dens, sign_ref, sign_sem):
    yl, xi, yh, z, core = (where_ref[k] for k in range(5))
    block_row = (yl * 4 + xi) * RB
    block_col = ((yh * 4 + z) * 2 + core) * QB
    same = lax.broadcasted_iota(jnp.int32, (BS, BS), 0) == lax.broadcasted_iota(jnp.int32, (BS, BS), 1)
    half_eye = jnp.where(same, 0.5, 0.0).astype(jnp.float32)

    def finish(i, carry):
        rows = pl.ds(pl.multiple_of(i * BS, BS), BS)
        for j in range(QB):
            cols = slice(j * BS, (j + 1) * BS)
            kept = jnp.where(pattern_ref[j, i] > 0, 0.5, 0.0)
            product = own_ref[rows, cols] + peer_ref[rows, cols]
            xnew = 1.5 * xm_ref[rows, cols].astype(jnp.float32) - kept * product
            sign_ref[rows, cols] = xnew.astype(jnp.bfloat16)
            on_diagonal = jnp.where(block_row + i == block_col + j, 1.0, 0.0)
            dens[i * QB + j] = (on_diagonal * half_eye - 0.5 * xnew).astype(jnp.bfloat16)
        return carry

    lax.fori_loop(0, RB, finish, 0)
    sign_copy = pltpu.make_async_copy(sign_ref, sign_out, sign_sem)
    sign_copy.start()
    dens[BLOCKS] = jnp.zeros((BS, BS), jnp.bfloat16)

    line = lax.broadcasted_iota(jnp.int32, (TAIL, BS), 0)

    def copy(owner, carry):
        energies = jnp.zeros((TAIL, BS), jnp.float32)
        for k in range(CAP):
            block = index_ref[owner * CAP + k]
            payload_ref[owner, k * BS : (k + 1) * BS, :] = dens[block]
            energies = jnp.where(line == k, energy_ref[block // QB], energies)
        payload_ref[owner, CAP * BS :, :] = energies.astype(jnp.bfloat16)
        return carry

    lax.fori_loop(0, payload_ref.shape[0], copy, 0, unroll=4)
    sign_copy.wait()


def finish_and_payload(where, pattern, index, energy, xm, own, peer):
    owners = index.shape[0] // CAP
    packet = (owners, CAP * BS + TAIL, BS)
    return pl.pallas_call(
        finish_kernel,
        in_specs=[SMEM] * 3 + [VMEM] * 4,
        out_specs=[HBM, VMEM],
        out_shape=[
            jax.ShapeDtypeStruct((ROWS, COLS), jnp.bfloat16),
            jax.ShapeDtypeStruct(packet, jnp.bfloat16),
        ],
        scratch_shapes=[
            pltpu.VMEM((BLOCKS + 1, BS, BS), jnp.bfloat16),
            pltpu.VMEM((ROWS, COLS), jnp.bfloat16),
            pltpu.SemaphoreType.DMA,
        ],
        compiler_params=pltpu.CompilerParams(vmem_limit_bytes=18 * 2**20),
        cost_estimate=pl.CostEstimate(flops=4 * ROWS * COLS, bytes_accessed=15 * 2**20, transcendentals=0),
        name="finish_payload",
    )(where, pattern, index, energy, xm, own, peer)


FCH = 16


def force_kernel(d_ref, h_ref, s_ref, out_ref, part_ref):
    same = lax.broadcasted_iota(jnp.int32, (BS, BS), 0) == lax.broadcasted_iota(jnp.int32, (BS, BS), 1)
    eye = jnp.where(same, 1.0, 0.0).astype(jnp.bfloat16)

    def group(i, carry):
        for j in range(FCH):
            source = i * FCH + j
            energies = d_ref[source, CAP * BS :, :].astype(jnp.float32)
            for k in range(CAP):
                slot = source * CAP + k
                spread = eye * energies[k : k + 1, :].astype(jnp.bfloat16)
                scaled = jnp.dot(spread, s_ref[slot], preferred_element_type=jnp.float32)
                term = d_ref[source, k * BS : (k + 1) * BS, :].astype(jnp.float32) * (
                    h_ref[slot].astype(jnp.float32) - scaled
                )
                row = j * CAP + k
                part_ref[i, row : row + 1, :] = jnp.sum(term, axis=0, keepdims=True)
        return carry

    lax.fori_loop(0, part_ref.shape[0], group, 0)
    parts = part_ref[...].reshape(out_ref.shape[0], BS)
    out_ref[...] = lax.dot_general(
        jnp.ones((8, BS), jnp.float32),
        parts,
        (((1,), (1,)), ((), ())),
        precision=lax.Precision.HIGHEST,
        preferred_element_type=jnp.float32,
    )[0]


def force_sums(packets, force_h, force_s):
    slots = force_h.shape[0]
    return pl.pallas_call(
        force_kernel,
        in_specs=[VMEM] * 3,
        out_specs=VMEM,
        out_shape=jax.ShapeDtypeStruct((slots,), jnp.float32),
        scratch_shapes=[pltpu.VMEM((slots // (FCH * CAP), FCH * CAP, BS), jnp.float32)],
        compiler_params=pltpu.CompilerParams(vmem_limit_bytes=12 * 2**20),
        cost_estimate=pl.CostEstimate(
            flops=6 * slots * BS * BS, bytes_accessed=6 * slots * BS * BS, transcendentals=0
        ),
        name="force_sums",
    )(packets, force_h, force_s)


def exchange(payload):
    return lax.all_to_all(payload, AXES, split_axis=0, concat_axis=0, tiled=True)


def shards(x, y, pattern_x, pattern_y, pattern_product, orbital_energy, pair_dest, pair_block, force_h, force_s):
    dest, wanted = pair_dest[0, :, 0], pair_block[0]
    slots = force_h.shape[0]
    entries = dest.shape[0]
    order = jnp.arange(entries, dtype=jnp.int32)
    earlier = (dest[:, None] == dest[None, :]) & (order[None, :] < order[:, None])
    rank = jnp.sum(earlier.astype(jnp.int32), axis=1)
    slot = dest * CAP + rank
    named = slot[None, :] == jnp.arange(slots, dtype=jnp.int32)[:, None]
    index = jnp.sum(jnp.where(named, wanted[None, :] - BLOCKS, 0), axis=1) + BLOCKS
    energy = jnp.pad(orbital_energy.astype(jnp.float32).reshape(RB, 1, BS), ((0, 1), (0, 0), (0, 0)))

    where = jnp.stack([lax.axis_index(axis) for axis in AXES]).astype(jnp.int32)
    half, quarter = ROWS // 2, ROWS // 4
    y_peer = lax.ppermute(y, "c", SWAP)
    pattern_peer = lax.ppermute(pattern_y.T, "c", SWAP)
    xm = mask_x(pattern_x.T, x)
    ym = mask_y(where, pattern_y.T, pattern_peer, y, y_peer)

    xm_z = after(xm, ym)
    xb_top = lax.ppermute(xm_z[:half], "yh", SWAP)
    xa_below = lax.ppermute(xm_z, "z", UP)
    xa_above = lax.ppermute(xm_z, "z", DOWN)
    ya_below = lax.ppermute(ym, "x", UP)
    ya_above = lax.ppermute(ym, "x", DOWN)
    yb = lax.ppermute(after(ym, xb_top), "yl", SWAP)
    xb_bottom = lax.ppermute(after(xm[half:], yb), "yh", SWAP)

    xa_far = [lax.ppermute(xa_below[:half], "z", UP), lax.ppermute(xa_above[half:], "z", DOWN)]
    ya_far = [lax.ppermute(ya_below[:quarter], "x", UP), lax.ppermute(ya_above[quarter:], "x", DOWN)]

    xb_top_z = after(xb_top, *xa_far)
    xbt_below, xbt_above = lax.ppermute(xb_top_z, "z", UP), lax.ppermute(xb_top_z, "z", DOWN)
    yb_x = after(yb, *ya_far)
    yb_below, yb_above = lax.ppermute(yb_x, "x", UP), lax.ppermute(yb_x, "x", DOWN)
    xb_bottom_z = after(xb_bottom, xbt_below, xbt_above)
    xbb_below, xbb_above = lax.ppermute(xb_bottom_z, "z", UP), lax.ppermute(xb_bottom_z, "z", DOWN)

    xb_far = [
        lax.ppermute(after(xbt_below, xbb_below), "z", UP),
        lax.ppermute(xbb_above, "z", DOWN),
    ]
    yb_far = [lax.ppermute(yb_below[:quarter], "x", UP), lax.ppermute(yb_above[quarter:], "x", DOWN)]

    x_parts = [xm, xa_below, xa_above, *xa_far, xb_top, xb_bottom, xbt_below, xbb_below, xbt_above, xbb_above]
    y_parts = [ym, ya_below, ya_above, *ya_far, yb, yb_below, yb_above]
    own, far, x_late, y_late = early_product(x_parts, y_parts, where)
    far = late_product(1, where, xb_far, yb_far, x_late, y_late, far)
    peer = lax.ppermute(far, "c", SWAP)
    own = late_product(0, where, xb_far, yb_far, x_late, y_late, after(own, far))
    sign_next, payload = finish_and_payload(where, pattern_product.T, index, energy, xm, own, peer)
    received = exchange(payload)
    return sign_next, force_sums(received, force_h, force_s)


def solution(mesh):
    fine = Mesh(mesh.devices.reshape(2, 4, 2, 4, 2), AXES)
    row, col = ("yl", "x"), ("yh", "z", "c")
    in_specs = (
        P(row, col),
        P(row, col),
        P(row, col),
        P(row, col),
        P(row, col),
        P(row),
        P(AXES, None, None),
        P(AXES, None),
        P(AXES, None, None),
        P(AXES, None, None),
    )
    out_specs = (P(row, col), P(AXES))
    return jax.shard_map(shards, mesh=fine, in_specs=in_specs, out_specs=out_specs, check_vma=False)
```

```python
import jax
import jax.numpy as jnp
from jax import lax
from jax.experimental import pallas as pl
from jax.experimental.pallas import tpu as pltpu
from jax.sharding import Mesh, PartitionSpec as P

BS = 128
QB = 4
CAP = 2
RB = 8
BLOCKS = RB * QB
TAIL = 8
SLOTS = 2 * CAP
ROWS = RB * BS
COLS = QB * BS
RING = 4
AXES = ("yl", "x", "yh", "z", "c")
SWAP = [(0, 1), (1, 0)]
UP = [(i, (i + 1) % RING) for i in range(RING)]
DOWN = [(i, (i - 1) % RING) for i in range(RING)]


def keep_block(pattern_ref, j, i):
    return (pattern_ref[j, i] > 0).astype(jnp.float32).astype(jnp.bfloat16)


def mask_x_kernel(p_ref, x_ref, o_ref):
    for i in range(RB):
        for j in range(QB):
            rows, cols = slice(i * BS, (i + 1) * BS), slice(j * BS, (j + 1) * BS)
            o_ref[rows, cols] = x_ref[rows, cols] * keep_block(p_ref, j, i)


def mask_y_kernel(where_ref, p_ref, q_ref, y_ref, z_ref, o_ref):
    first = where_ref[4] * (RB // 2)
    for i in range(RB // 2):
        rows = slice(i * BS, (i + 1) * BS)
        own_rows = pl.ds(pl.multiple_of((first + i) * BS, BS), BS)
        for j in range(QB):
            cols = slice(j * BS, (j + 1) * BS)
            far_cols = slice(COLS + j * BS, COLS + (j + 1) * BS)
            o_ref[rows, cols] = y_ref[own_rows, cols] * keep_block(p_ref, j, first + i)
            o_ref[rows, far_cols] = z_ref[own_rows, cols] * keep_block(q_ref, j, first + i)


SMEM = pl.BlockSpec(memory_space=pltpu.SMEM)
VMEM = pl.BlockSpec(memory_space=pltpu.VMEM)
HBM = pl.BlockSpec(memory_space=pltpu.HBM)


def mask_x(pattern, x):
    return pl.pallas_call(
        mask_x_kernel,
        in_specs=[SMEM, VMEM],
        out_specs=VMEM,
        out_shape=jax.ShapeDtypeStruct((ROWS, COLS), jnp.bfloat16),
        compiler_params=pltpu.CompilerParams(vmem_limit_bytes=8 * 2**20),
        cost_estimate=pl.CostEstimate(flops=ROWS * COLS, bytes_accessed=4 * ROWS * COLS, transcendentals=0),
        name="mask_x",
    )(pattern, x)


def mask_y(where, pattern, pattern_peer, y, y_peer):
    return pl.pallas_call(
        mask_y_kernel,
        in_specs=[SMEM] * 3 + [VMEM] * 2,
        out_specs=VMEM,
        out_shape=jax.ShapeDtypeStruct((ROWS // 2, 2 * COLS), jnp.bfloat16),
        compiler_params=pltpu.CompilerParams(vmem_limit_bytes=8 * 2**20),
        cost_estimate=pl.CostEstimate(flops=ROWS * COLS, bytes_accessed=6 * ROWS * COLS, transcendentals=0),
        name="mask_y",
    )(where, pattern, pattern_peer, y, y_peer)


def after(value, *others):
    return lax.optimization_barrier((value,) + others)[0]


def y_place(where_ref, position):
    yl, xi, yh, z = (where_ref[k] for k in range(4))
    member = position % 4
    offset = jnp.where(member == 0, 0, jnp.where(member == 1, 3, jnp.where(member == 2, 1, 2)))
    gap = (z + offset - xi + 2 * RING) % RING
    y_member = jnp.where(gap == 0, 0, jnp.where(gap == 3, 1, jnp.where(gap == 1, 2, 3)))
    return (yh ^ (position // 4) ^ yl) * 4 + y_member


X_PIECES = ((0, 0, 2), (1, 0, 2), (2, 0, 2), (3, 0, 1), (3, 1, 1), (4, 0, 1), (4, 1, 1), (5, 0, 1), (5, 1, 1), (6, 0, 1), (6, 1, 1))
Y_PIECES = ((0, 0, 2), (1, 0, 2), (2, 0, 2), (3, 0, 1), (3, 1, 1), (4, 0, 2), (5, 0, 2), (6, 0, 2))
EARLY = 7


def early_kernel(*refs):
    nx, ny = len(X_PIECES), len(Y_PIECES)
    x_in, y_in, where_ref = refs[:nx], refs[nx : nx + ny], refs[nx + ny]
    own_ref, far_ref, x_late, y_late = refs[nx + ny + 1 : nx + ny + 5]
    x_buf, y_buf, x_sem, y_sem = refs[nx + ny + 5 :]

    for k in range(max(nx, ny)):
        for pieces, source, buf, sem, half in (
            (X_PIECES, x_in, x_buf, x_sem, ROWS // 2),
            (Y_PIECES, y_in, y_buf, y_sem, ROWS // 4),
        ):
            if k < len(pieces):
                position, start, size = pieces[k]
                target = buf.at[position, pl.ds(start * half, size * half)]
                pltpu.make_async_copy(source[k], target, sem.at[position]).start()

    own_ref[...] = jnp.zeros_like(own_ref)
    far_ref[...] = jnp.zeros_like(far_ref)

    def step(position, carry):
        pltpu.make_async_copy(x_buf.at[position], x_buf.at[position], x_sem.at[position]).wait()
        y_position = y_place(where_ref, position)

        @pl.when(y_position != EARLY)
        def _():
            pltpu.make_async_copy(y_buf.at[y_position], y_buf.at[y_position], y_sem.at[y_position]).wait()
            for out_ref, cols in ((own_ref, slice(0, COLS)), (far_ref, slice(COLS, 2 * COLS))):
                out_ref[...] += jnp.dot(
                    x_buf[position], y_buf[y_position, :, cols], preferred_element_type=jnp.float32
                )

        @pl.when(y_position == EARLY)
        def _():
            x_late[...] = x_buf[position]

        return carry

    lax.fori_loop(0, EARLY, step, 0)
    last = y_place(where_ref, EARLY)

    @pl.when(last != EARLY)
    def _():
        pltpu.make_async_copy(y_buf.at[last], y_buf.at[last], y_sem.at[last]).wait()
        y_late[...] = y_buf[last]


def early_product(x_parts, y_parts, where):
    return pl.pallas_call(
        early_kernel,
        in_specs=[HBM] * (len(X_PIECES) + len(Y_PIECES)) + [SMEM],
        out_specs=[VMEM] * 4,
        out_shape=[
            jax.ShapeDtypeStruct((ROWS, COLS), jnp.float32),
            jax.ShapeDtypeStruct((ROWS, COLS), jnp.float32),
            jax.ShapeDtypeStruct((ROWS, COLS), jnp.bfloat16),
            jax.ShapeDtypeStruct((ROWS // 2, 2 * COLS), jnp.bfloat16),
        ],
        scratch_shapes=[
            pltpu.VMEM((EARLY, ROWS, COLS), jnp.bfloat16),
            pltpu.VMEM((EARLY, ROWS // 2, 2 * COLS), jnp.bfloat16),
            pltpu.SemaphoreType.DMA((EARLY,)),
            pltpu.SemaphoreType.DMA((EARLY,)),
        ],
        compiler_params=pltpu.CompilerParams(vmem_limit_bytes=24 * 2**20),
        cost_estimate=pl.CostEstimate(
            flops=14 * ROWS * COLS * ROWS, bytes_accessed=20 * 2**20, transcendentals=0
        ),
        name="early_product",
    )(*x_parts, *y_parts, where)


def late_kernel(where_ref, x_top, x_bottom, y_top, y_bottom, x_late, y_late, sum_ref, out_ref):
    last = y_place(where_ref, EARLY)
    quarter = ROWS // 4

    def add(x_far, same_chunk):
        x_last = x_far if same_chunk else x_late
        total = sum_ref[...]
        total += jnp.dot(x_last[:, :quarter], y_top[...], preferred_element_type=jnp.float32)
        total += jnp.dot(x_last[:, quarter:], y_bottom[...], preferred_element_type=jnp.float32)
        if not same_chunk:
            total += jnp.dot(x_far[...], y_late[...], preferred_element_type=jnp.float32)
        out_ref[...] = total

    for upper, x_far in ((True, x_top), (False, x_bottom)):
        for same_chunk in (True, False):
            here = (pl.program_id(0) < 1) == upper
            pl.when(here & ((last == EARLY) == same_chunk))(lambda x=x_far, t=same_chunk: add(x, t))


def late_product(side, where, x_far, y_far, x_late, y_late, total):
    half, quarter = ROWS // 2, ROWS // 4
    rows = pl.BlockSpec((half, COLS), lambda m: (m, 0))
    whole = pl.BlockSpec((half, COLS), lambda m: (0, 0))

    def columns(height):
        return pl.BlockSpec((height, COLS), lambda m: (0, side))

    return pl.pallas_call(
        late_kernel,
        grid=(2,),
        in_specs=[SMEM, whole, whole, columns(quarter), columns(quarter), rows, columns(half), rows],
        out_specs=rows,
        out_shape=jax.ShapeDtypeStruct((ROWS, COLS), jnp.float32),
        compiler_params=pltpu.CompilerParams(vmem_limit_bytes=16 * 2**20),
        cost_estimate=pl.CostEstimate(
            flops=2 * ROWS * COLS * ROWS, bytes_accessed=8 * 2**20, transcendentals=0
        ),
        name="late_product",
    )(where, *x_far, *y_far, x_late, y_late, total)


def finish_kernel(where_ref, pattern_ref, xm_ref, own_ref, peer_ref, sign_ref, dens_ref):
    yl, xi, yh, z, core = (where_ref[k] for k in range(5))
    block_row = (yl * 4 + xi) * RB
    block_col = ((yh * 4 + z) * 2 + core) * QB
    same = lax.broadcasted_iota(jnp.int32, (BS, BS), 0) == lax.broadcasted_iota(jnp.int32, (BS, BS), 1)
    half_eye = jnp.where(same, 0.5, 0.0).astype(jnp.float32)

    def finish(i, carry):
        rows = pl.ds(pl.multiple_of(i * BS, BS), BS)
        for j in range(QB):
            cols = slice(j * BS, (j + 1) * BS)
            kept = jnp.where(pattern_ref[j, i] > 0, 0.5, 0.0)
            product = own_ref[rows, cols] + peer_ref[rows, cols]
            xnew = 1.5 * xm_ref[rows, cols].astype(jnp.float32) - kept * product
            sign_ref[rows, cols] = xnew.astype(jnp.bfloat16)
            on_diagonal = jnp.where(block_row + i == block_col + j, 1.0, 0.0)
            dens_ref[i * QB + j] = (on_diagonal * half_eye - 0.5 * xnew).astype(jnp.bfloat16)
        return carry

    lax.fori_loop(0, RB, finish, 0)
    dens_ref[BLOCKS] = jnp.zeros((BS, BS), jnp.bfloat16)


def finish_tile(where, pattern, xm, own, peer):
    return pl.pallas_call(
        finish_kernel,
        in_specs=[SMEM] * 2 + [VMEM] * 3,
        out_specs=[VMEM] * 2,
        out_shape=[
            jax.ShapeDtypeStruct((ROWS, COLS), jnp.bfloat16),
            jax.ShapeDtypeStruct((BLOCKS + 1, BS, BS), jnp.bfloat16),
        ],
        compiler_params=pltpu.CompilerParams(vmem_limit_bytes=18 * 2**20),
        cost_estimate=pl.CostEstimate(flops=4 * ROWS * COLS, bytes_accessed=9 * 2**20, transcendentals=0),
        name="finish_tile",
    )(where, pattern, xm, own, peer)


def pack_kernel(where_ref, own_index, peer_index, energy_ref, own_dens, peer_dens, sign_ref, sign_out, payload_ref, sem):
    core = where_ref[4]
    sign_copy = pltpu.make_async_copy(sign_ref, sign_out, sem)
    sign_copy.start()
    line = lax.broadcasted_iota(jnp.int32, (TAIL, BS), 0)

    def copy(chip, carry):
        energies = jnp.zeros((TAIL, BS), jnp.float32)
        for index_ref, dens_ref, source in ((own_index, own_dens, core), (peer_index, peer_dens, 1 - core)):
            for k in range(CAP):
                block = index_ref[(chip * 2 + core) * CAP + k]
                place = source * CAP + k
                payload_ref[chip, pl.ds(pl.multiple_of(place * BS, BS), BS), :] = dens_ref[block]
                energies = jnp.where(line == place, energy_ref[block // QB], energies)
        payload_ref[chip, SLOTS * BS :, :] = energies.astype(jnp.bfloat16)
        return carry

    lax.fori_loop(0, payload_ref.shape[0], copy, 0, unroll=2)
    sign_copy.wait()


def pack(where, own_index, peer_index, energy, own_dens, peer_dens, sign):
    chips = own_index.shape[0] // SLOTS
    return pl.pallas_call(
        pack_kernel,
        in_specs=[SMEM] * 3 + [VMEM] * 4,
        out_specs=[HBM, VMEM],
        out_shape=[
            jax.ShapeDtypeStruct((ROWS, COLS), jnp.bfloat16),
            jax.ShapeDtypeStruct((chips, SLOTS * BS + TAIL, BS), jnp.bfloat16),
        ],
        scratch_shapes=[pltpu.SemaphoreType.DMA],
        compiler_params=pltpu.CompilerParams(vmem_limit_bytes=16 * 2**20),
        cost_estimate=pl.CostEstimate(flops=ROWS * COLS, bytes_accessed=12 * 2**20, transcendentals=0),
        name="pack_payload",
    )(where, own_index, peer_index, energy, own_dens, peer_dens, sign)


FCH = 8


def force_kernel(d_ref, h_ref, s_ref, out_ref, part_ref):
    same = lax.broadcasted_iota(jnp.int32, (BS, BS), 0) == lax.broadcasted_iota(jnp.int32, (BS, BS), 1)
    eye = jnp.where(same, 1.0, 0.0).astype(jnp.bfloat16)

    def group(i, carry):
        for j in range(FCH):
            source = i * FCH + j
            energies = d_ref[source, SLOTS * BS :, :].astype(jnp.float32)
            for k in range(SLOTS):
                slot = source * SLOTS + k
                spread = eye * energies[k : k + 1, :].astype(jnp.bfloat16)
                scaled = jnp.dot(spread, s_ref[slot], preferred_element_type=jnp.float32)
                term = d_ref[source, k * BS : (k + 1) * BS, :].astype(jnp.float32) * (
                    h_ref[slot].astype(jnp.float32) - scaled
                )
                row = j * SLOTS + k
                part_ref[i, row : row + 1, :] = jnp.sum(term, axis=0, keepdims=True)
        return carry

    lax.fori_loop(0, part_ref.shape[0], group, 0)
    parts = part_ref[...].reshape(out_ref.shape[0], BS)
    out_ref[...] = lax.dot_general(
        jnp.ones((8, BS), jnp.float32),
        parts,
        (((1,), (1,)), ((), ())),
        precision=lax.Precision.HIGHEST,
        preferred_element_type=jnp.float32,
    )[0]


def force_sums(packets, force_h, force_s):
    slots = force_h.shape[0]
    return pl.pallas_call(
        force_kernel,
        in_specs=[VMEM] * 3,
        out_specs=VMEM,
        out_shape=jax.ShapeDtypeStruct((slots,), jnp.float32),
        scratch_shapes=[pltpu.VMEM((slots // (FCH * SLOTS), FCH * SLOTS, BS), jnp.float32)],
        compiler_params=pltpu.CompilerParams(vmem_limit_bytes=12 * 2**20),
        cost_estimate=pl.CostEstimate(
            flops=6 * slots * BS * BS, bytes_accessed=6 * slots * BS * BS, transcendentals=0
        ),
        name="force_sums",
    )(packets, force_h, force_s)


def exchange(payload):
    return lax.all_to_all(payload, AXES[:4], split_axis=0, concat_axis=0, tiled=True)


def shards(x, y, pattern_x, pattern_y, pattern_product, orbital_energy, pair_dest, pair_block, force_h, force_s):
    dest, wanted = pair_dest[0, :, 0], pair_block[0]
    slots = force_h.shape[0]
    entries = dest.shape[0]
    order = jnp.arange(entries, dtype=jnp.int32)
    earlier = (dest[:, None] == dest[None, :]) & (order[None, :] < order[:, None])
    rank = jnp.sum(earlier.astype(jnp.int32), axis=1)
    slot = dest * CAP + rank
    named = slot[None, :] == jnp.arange(slots, dtype=jnp.int32)[:, None]
    index = jnp.sum(jnp.where(named, wanted[None, :] - BLOCKS, 0), axis=1) + BLOCKS
    energy = jnp.pad(orbital_energy.astype(jnp.float32).reshape(RB, 1, BS), ((0, 1), (0, 0), (0, 0)))

    where = jnp.stack([lax.axis_index(axis) for axis in AXES]).astype(jnp.int32)
    half, quarter = ROWS // 2, ROWS // 4
    y_peer = lax.ppermute(y, "c", SWAP)
    peer_index = lax.ppermute(index, "c", SWAP)
    pattern_peer = lax.ppermute(pattern_y.T, "c", SWAP)
    xm = mask_x(pattern_x.T, x)
    ym = mask_y(where, pattern_y.T, pattern_peer, y, y_peer)

    xm_z = after(xm, ym)
    xb_top = lax.ppermute(xm_z[:half], "yh", SWAP)
    xa_below = lax.ppermute(xm_z, "z", UP)
    xa_above = lax.ppermute(xm_z, "z", DOWN)
    ya_below = lax.ppermute(ym, "x", UP)
    ya_above = lax.ppermute(ym, "x", DOWN)
    yb = lax.ppermute(after(ym, xb_top), "yl", SWAP)
    xb_bottom = lax.ppermute(after(xm[half:], yb), "yh", SWAP)

    xa_far = [lax.ppermute(xa_below[:half], "z", UP), lax.ppermute(xa_above[half:], "z", DOWN)]
    ya_far = [lax.ppermute(ya_below[:quarter], "x", UP), lax.ppermute(ya_above[quarter:], "x", DOWN)]

    xb_top_z = after(xb_top, *xa_far)
    xbt_below, xbt_above = lax.ppermute(xb_top_z, "z", UP), lax.ppermute(xb_top_z, "z", DOWN)
    yb_x = after(yb, *ya_far)
    yb_below, yb_above = lax.ppermute(yb_x, "x", UP), lax.ppermute(yb_x, "x", DOWN)
    xb_bottom_z = after(xb_bottom, xbt_below, xbt_above)
    xbb_below, xbb_above = lax.ppermute(xb_bottom_z, "z", UP), lax.ppermute(xb_bottom_z, "z", DOWN)

    xb_far = [
        lax.ppermute(after(xbt_below, xbb_below), "z", UP),
        lax.ppermute(xbb_above, "z", DOWN),
    ]
    yb_far = [lax.ppermute(yb_below[:quarter], "x", UP), lax.ppermute(yb_above[quarter:], "x", DOWN)]

    x_parts = [xm, xa_below, xa_above, *xa_far, xb_top, xb_bottom, xbt_below, xbb_below, xbt_above, xbb_above]
    y_parts = [ym, ya_below, ya_above, *ya_far, yb, yb_below, yb_above]
    own, far, x_late, y_late = early_product(x_parts, y_parts, after(where, peer_index))
    far = late_product(1, where, xb_far, yb_far, x_late, y_late, far)
    peer = lax.ppermute(far, "c", SWAP)
    own = late_product(0, where, xb_far, yb_far, x_late, y_late, after(own, far))
    sign, dens = finish_tile(where, pattern_product.T, xm, own, peer)
    peer_dens = lax.ppermute(dens, "c", SWAP)
    sign_next, payload = pack(where, index, peer_index, energy, dens, peer_dens, sign)
    received = exchange(payload)
    return sign_next, force_sums(received, force_h, force_s)


def solution(mesh):
    fine = Mesh(mesh.devices.reshape(2, 4, 2, 4, 2), AXES)
    row, col = ("yl", "x"), ("yh", "z", "c")
    in_specs = (
        P(row, col),
        P(row, col),
        P(row, col),
        P(row, col),
        P(row, col),
        P(row),
        P(AXES, None, None),
        P(AXES, None),
        P(AXES, None, None),
        P(AXES, None, None),
    )
    out_specs = (P(row, col), P(AXES))
    return jax.shard_map(shards, mesh=fine, in_specs=in_specs, out_specs=out_specs, check_vma=False)
```

```python
import jax
import jax.numpy as jnp
from jax import lax
from jax.experimental import pallas as pl
from jax.experimental.pallas import tpu as pltpu
from jax.sharding import Mesh, PartitionSpec as P

BS = 128
QB = 4
CAP = 2
RB = 8
BLOCKS = RB * QB
TAIL = 8
ROWS = RB * BS
COLS = QB * BS
RING = 4
AXES = ("yl", "x", "yh", "z", "c")
SWAP = [(0, 1), (1, 0)]
UP = [(i, (i + 1) % RING) for i in range(RING)]
DOWN = [(i, (i - 1) % RING) for i in range(RING)]


def keep_block(pattern_ref, j, i):
    return (pattern_ref[j, i] > 0).astype(jnp.float32).astype(jnp.bfloat16)


def mask_x_kernel(p_ref, x_ref, o_ref):
    for i in range(RB):
        for j in range(QB):
            rows, cols = slice(i * BS, (i + 1) * BS), slice(j * BS, (j + 1) * BS)
            o_ref[rows, cols] = x_ref[rows, cols] * keep_block(p_ref, j, i)


def mask_y_kernel(where_ref, p_ref, q_ref, y_ref, z_ref, o_ref):
    first = where_ref[4] * (RB // 2)
    for i in range(RB // 2):
        rows = slice(i * BS, (i + 1) * BS)
        own_rows = pl.ds(pl.multiple_of((first + i) * BS, BS), BS)
        for j in range(QB):
            cols = slice(j * BS, (j + 1) * BS)
            far_cols = slice(COLS + j * BS, COLS + (j + 1) * BS)
            o_ref[rows, cols] = y_ref[own_rows, cols] * keep_block(p_ref, j, first + i)
            o_ref[rows, far_cols] = z_ref[own_rows, cols] * keep_block(q_ref, j, first + i)


SMEM = pl.BlockSpec(memory_space=pltpu.SMEM)
VMEM = pl.BlockSpec(memory_space=pltpu.VMEM)
HBM = pl.BlockSpec(memory_space=pltpu.HBM)


def mask_x(pattern, x):
    return pl.pallas_call(
        mask_x_kernel,
        in_specs=[SMEM, VMEM],
        out_specs=VMEM,
        out_shape=jax.ShapeDtypeStruct((ROWS, COLS), jnp.bfloat16),
        compiler_params=pltpu.CompilerParams(vmem_limit_bytes=8 * 2**20),
        cost_estimate=pl.CostEstimate(flops=ROWS * COLS, bytes_accessed=4 * ROWS * COLS, transcendentals=0),
        name="mask_x",
    )(pattern, x)


def mask_y(where, pattern, pattern_peer, y, y_peer):
    return pl.pallas_call(
        mask_y_kernel,
        in_specs=[SMEM] * 3 + [VMEM] * 2,
        out_specs=VMEM,
        out_shape=jax.ShapeDtypeStruct((ROWS // 2, 2 * COLS), jnp.bfloat16),
        compiler_params=pltpu.CompilerParams(vmem_limit_bytes=8 * 2**20),
        cost_estimate=pl.CostEstimate(flops=ROWS * COLS, bytes_accessed=6 * ROWS * COLS, transcendentals=0),
        name="mask_y",
    )(where, pattern, pattern_peer, y, y_peer)


def after(value, *others):
    return lax.optimization_barrier((value,) + others)[0]


def y_place(where_ref, position):
    yl, xi, yh, z = (where_ref[k] for k in range(4))
    member = position % 4
    offset = jnp.where(member == 0, 0, jnp.where(member == 1, 3, jnp.where(member == 2, 1, 2)))
    gap = (z + offset - xi + 2 * RING) % RING
    y_member = jnp.where(gap == 0, 0, jnp.where(gap == 3, 1, jnp.where(gap == 1, 2, 3)))
    return (yh ^ (position // 4) ^ yl) * 4 + y_member


X_PIECES = ((0, 0, 2), (1, 0, 2), (2, 0, 2), (3, 0, 1), (3, 1, 1), (4, 0, 1), (4, 1, 1), (5, 0, 1), (5, 1, 1), (6, 0, 1), (6, 1, 1))
Y_PIECES = ((0, 0, 2), (1, 0, 2), (2, 0, 2), (3, 0, 1), (3, 1, 1), (4, 0, 2), (5, 0, 2), (6, 0, 2))
EARLY = 7


def early_kernel(*refs):
    nx, ny = len(X_PIECES), len(Y_PIECES)
    x_in, y_in, where_ref = refs[:nx], refs[nx : nx + ny], refs[nx + ny]
    own_ref, far_ref, x_late, y_late = refs[nx + ny + 1 : nx + ny + 5]
    y_buf, y_sem = refs[nx + ny + 5 :]
    half = ROWS // 2

    for k, (position, start, size) in enumerate(Y_PIECES):
        target = y_buf.at[position, pl.ds(start * (half // 2), size * (half // 2))]
        pltpu.make_async_copy(y_in[k], target, y_sem.at[position]).start()

    own_ref[...] = jnp.zeros_like(own_ref)
    far_ref[...] = jnp.zeros_like(far_ref)

    def x_halves(position):
        pieces = [(x_in[k], piece) for k, piece in enumerate(X_PIECES) if piece[0] == position]
        if len(pieces) == 1:
            return [pieces[0][0].at[pl.ds(part * half, half)] for part in range(2)]
        return [ref for ref, _ in pieces]

    for position in range(EARLY):
        y_position = y_place(where_ref, position)
        halves = x_halves(position)

        @pl.when(y_position != EARLY)
        def _():
            pltpu.make_async_copy(y_buf.at[y_position], y_buf.at[y_position], y_sem.at[y_position]).wait()
            for part, x_ref in enumerate(halves):
                rows = slice(part * half, (part + 1) * half)
                for out_ref, cols in ((own_ref, slice(0, COLS)), (far_ref, slice(COLS, 2 * COLS))):
                    out_ref[rows, :] += jnp.dot(
                        x_ref[...], y_buf[y_position, :, cols], preferred_element_type=jnp.float32
                    )

        @pl.when(y_position == EARLY)
        def _():
            for part, x_ref in enumerate(halves):
                x_late[slice(part * half, (part + 1) * half), :] = x_ref[...]

    last = y_place(where_ref, EARLY)

    @pl.when(last != EARLY)
    def _():
        pltpu.make_async_copy(y_buf.at[last], y_buf.at[last], y_sem.at[last]).wait()
        y_late[...] = y_buf[last]


def early_product(x_parts, y_parts, where):
    return pl.pallas_call(
        early_kernel,
        in_specs=[VMEM] * len(X_PIECES) + [HBM] * len(Y_PIECES) + [SMEM],
        out_specs=[VMEM] * 4,
        out_shape=[
            jax.ShapeDtypeStruct((ROWS, COLS), jnp.float32),
            jax.ShapeDtypeStruct((ROWS, COLS), jnp.float32),
            jax.ShapeDtypeStruct((ROWS, COLS), jnp.bfloat16),
            jax.ShapeDtypeStruct((ROWS // 2, 2 * COLS), jnp.bfloat16),
        ],
        scratch_shapes=[
            pltpu.VMEM((EARLY, ROWS // 2, 2 * COLS), jnp.bfloat16),
            pltpu.SemaphoreType.DMA((EARLY,)),
        ],
        compiler_params=pltpu.CompilerParams(vmem_limit_bytes=24 * 2**20),
        cost_estimate=pl.CostEstimate(
            flops=14 * ROWS * COLS * ROWS, bytes_accessed=20 * 2**20, transcendentals=0
        ),
        name="early_product",
    )(*x_parts, *y_parts, where)


def late_kernel(where_ref, x_top, x_bottom, y_top, y_bottom, x_late, y_late, sum_ref, out_ref):
    last = y_place(where_ref, EARLY)
    quarter = ROWS // 4

    def add(x_far, same_chunk):
        x_last = x_far if same_chunk else x_late
        total = sum_ref[...]
        total += jnp.dot(x_last[:, :quarter], y_top[...], preferred_element_type=jnp.float32)
        total += jnp.dot(x_last[:, quarter:], y_bottom[...], preferred_element_type=jnp.float32)
        if not same_chunk:
            total += jnp.dot(x_far[...], y_late[...], preferred_element_type=jnp.float32)
        out_ref[...] = total

    for upper, x_far in ((True, x_top), (False, x_bottom)):
        for same_chunk in (True, False):
            here = (pl.program_id(0) < 1) == upper
            pl.when(here & ((last == EARLY) == same_chunk))(lambda x=x_far, t=same_chunk: add(x, t))


def late_product(side, where, x_far, y_far, x_late, y_late, total):
    half, quarter = ROWS // 2, ROWS // 4
    rows = pl.BlockSpec((half, COLS), lambda m: (m, 0))
    whole = pl.BlockSpec((half, COLS), lambda m: (0, 0))

    def columns(height):
        return pl.BlockSpec((height, COLS), lambda m: (0, side))

    return pl.pallas_call(
        late_kernel,
        grid=(2,),
        in_specs=[SMEM, whole, whole, columns(quarter), columns(quarter), rows, columns(half), rows],
        out_specs=rows,
        out_shape=jax.ShapeDtypeStruct((ROWS, COLS), jnp.float32),
        compiler_params=pltpu.CompilerParams(vmem_limit_bytes=16 * 2**20),
        cost_estimate=pl.CostEstimate(
            flops=2 * ROWS * COLS * ROWS, bytes_accessed=8 * 2**20, transcendentals=0
        ),
        name="late_product",
    )(where, *x_far, *y_far, x_late, y_late, total)


def finish_kernel(where_ref, pattern_ref, index_ref, energy_ref, xm_ref, own_ref, peer_ref, sign_out, payload_ref, dens, sign_ref, sign_sem):
    yl, xi, yh, z, core = (where_ref[k] for k in range(5))
    block_row = (yl * 4 + xi) * RB
    block_col = ((yh * 4 + z) * 2 + core) * QB
    same = lax.broadcasted_iota(jnp.int32, (BS, BS), 0) == lax.broadcasted_iota(jnp.int32, (BS, BS), 1)
    half_eye = jnp.where(same, 0.5, 0.0).astype(jnp.float32)

    def finish(i, carry):
        rows = pl.ds(pl.multiple_of(i * BS, BS), BS)
        for j in range(QB):
            cols = slice(j * BS, (j + 1) * BS)
            kept = jnp.where(pattern_ref[j, i] > 0, 0.5, 0.0)
            product = own_ref[rows, cols] + peer_ref[rows, cols]
            xnew = 1.5 * xm_ref[rows, cols].astype(jnp.float32) - kept * product
            sign_ref[rows, cols] = xnew.astype(jnp.bfloat16)
            on_diagonal = jnp.where(block_row + i == block_col + j, 1.0, 0.0)
            dens[i * QB + j] = (on_diagonal * half_eye - 0.5 * xnew).astype(jnp.bfloat16)
        return carry

    lax.fori_loop(0, RB, finish, 0)
    sign_copy = pltpu.make_async_copy(sign_ref, sign_out, sign_sem)
    sign_copy.start()
    dens[BLOCKS] = jnp.zeros((BS, BS), jnp.bfloat16)

    line = lax.broadcasted_iota(jnp.int32, (TAIL, BS), 0)

    def copy(owner, carry):
        energies = jnp.zeros((TAIL, BS), jnp.float32)
        for k in range(CAP):
            block = index_ref[owner * CAP + k]
            payload_ref[owner, k * BS : (k + 1) * BS, :] = dens[block]
            energies = jnp.where(line == k, energy_ref[block // QB], energies)
        payload_ref[owner, CAP * BS :, :] = energies.astype(jnp.bfloat16)
        return carry

    lax.fori_loop(0, payload_ref.shape[0], copy, 0, unroll=4)
    sign_copy.wait()


def finish_and_payload(where, pattern, index, energy, xm, own, peer):
    owners = index.shape[0] // CAP
    packet = (owners, CAP * BS + TAIL, BS)
    return pl.pallas_call(
        finish_kernel,
        in_specs=[SMEM] * 3 + [VMEM] * 4,
        out_specs=[HBM, VMEM],
        out_shape=[
            jax.ShapeDtypeStruct((ROWS, COLS), jnp.bfloat16),
            jax.ShapeDtypeStruct(packet, jnp.bfloat16),
        ],
        scratch_shapes=[
            pltpu.VMEM((BLOCKS + 1, BS, BS), jnp.bfloat16),
            pltpu.VMEM((ROWS, COLS), jnp.bfloat16),
            pltpu.SemaphoreType.DMA,
        ],
        compiler_params=pltpu.CompilerParams(vmem_limit_bytes=18 * 2**20),
        cost_estimate=pl.CostEstimate(flops=4 * ROWS * COLS, bytes_accessed=15 * 2**20, transcendentals=0),
        name="finish_payload",
    )(where, pattern, index, energy, xm, own, peer)


FCH = 16


def force_kernel(d_ref, h_ref, s_ref, out_ref, part_ref):
    same = lax.broadcasted_iota(jnp.int32, (BS, BS), 0) == lax.broadcasted_iota(jnp.int32, (BS, BS), 1)
    eye = jnp.where(same, 1.0, 0.0).astype(jnp.bfloat16)

    def group(i, carry):
        for j in range(FCH):
            source = i * FCH + j
            energies = d_ref[source, CAP * BS :, :].astype(jnp.float32)
            for k in range(CAP):
                slot = source * CAP + k
                spread = eye * energies[k : k + 1, :].astype(jnp.bfloat16)
                scaled = jnp.dot(spread, s_ref[slot], preferred_element_type=jnp.float32)
                term = d_ref[source, k * BS : (k + 1) * BS, :].astype(jnp.float32) * (
                    h_ref[slot].astype(jnp.float32) - scaled
                )
                row = j * CAP + k
                part_ref[i, row : row + 1, :] = jnp.sum(term, axis=0, keepdims=True)
        return carry

    lax.fori_loop(0, part_ref.shape[0], group, 0)
    parts = part_ref[...].reshape(out_ref.shape[0], BS)
    out_ref[...] = lax.dot_general(
        jnp.ones((8, BS), jnp.float32),
        parts,
        (((1,), (1,)), ((), ())),
        precision=lax.Precision.HIGHEST,
        preferred_element_type=jnp.float32,
    )[0]


def force_sums(packets, force_h, force_s):
    slots = force_h.shape[0]
    return pl.pallas_call(
        force_kernel,
        in_specs=[VMEM] * 3,
        out_specs=VMEM,
        out_shape=jax.ShapeDtypeStruct((slots,), jnp.float32),
        scratch_shapes=[pltpu.VMEM((slots // (FCH * CAP), FCH * CAP, BS), jnp.float32)],
        compiler_params=pltpu.CompilerParams(vmem_limit_bytes=12 * 2**20),
        cost_estimate=pl.CostEstimate(
            flops=6 * slots * BS * BS, bytes_accessed=6 * slots * BS * BS, transcendentals=0
        ),
        name="force_sums",
    )(packets, force_h, force_s)


def exchange(payload):
    return lax.all_to_all(payload, AXES, split_axis=0, concat_axis=0, tiled=True)


def shards(x, y, pattern_x, pattern_y, pattern_product, orbital_energy, pair_dest, pair_block, force_h, force_s):
    dest, wanted = pair_dest[0, :, 0], pair_block[0]
    slots = force_h.shape[0]
    entries = dest.shape[0]
    order = jnp.arange(entries, dtype=jnp.int32)
    earlier = (dest[:, None] == dest[None, :]) & (order[None, :] < order[:, None])
    rank = jnp.sum(earlier.astype(jnp.int32), axis=1)
    slot = dest * CAP + rank
    named = slot[None, :] == jnp.arange(slots, dtype=jnp.int32)[:, None]
    index = jnp.sum(jnp.where(named, wanted[None, :] - BLOCKS, 0), axis=1) + BLOCKS
    energy = jnp.pad(orbital_energy.astype(jnp.float32).reshape(RB, 1, BS), ((0, 1), (0, 0), (0, 0)))

    where = jnp.stack([lax.axis_index(axis) for axis in AXES]).astype(jnp.int32)
    half, quarter = ROWS // 2, ROWS // 4
    y_peer = lax.ppermute(y, "c", SWAP)
    pattern_peer = lax.ppermute(pattern_y.T, "c", SWAP)
    xm = mask_x(pattern_x.T, x)
    ym = mask_y(where, pattern_y.T, pattern_peer, y, y_peer)

    xm_z = after(xm, ym)
    xb_top = lax.ppermute(xm_z[:half], "yh", SWAP)
    xa_below = lax.ppermute(xm_z, "z", UP)
    xa_above = lax.ppermute(xm_z, "z", DOWN)
    ya_below = lax.ppermute(ym, "x", UP)
    ya_above = lax.ppermute(ym, "x", DOWN)
    yb = lax.ppermute(after(ym, xb_top), "yl", SWAP)
    xb_bottom = lax.ppermute(after(xm[half:], yb), "yh", SWAP)

    xa_far = [lax.ppermute(xa_below[:half], "z", UP), lax.ppermute(xa_above[half:], "z", DOWN)]
    ya_far = [lax.ppermute(ya_below[:quarter], "x", UP), lax.ppermute(ya_above[quarter:], "x", DOWN)]

    xb_top_z = after(xb_top, *xa_far)
    xbt_below, xbt_above = lax.ppermute(xb_top_z, "z", UP), lax.ppermute(xb_top_z, "z", DOWN)
    yb_x = after(yb, *ya_far)
    yb_below, yb_above = lax.ppermute(yb_x, "x", UP), lax.ppermute(yb_x, "x", DOWN)
    xb_bottom_z = after(xb_bottom, xbt_below, xbt_above)
    xbb_below, xbb_above = lax.ppermute(xb_bottom_z, "z", UP), lax.ppermute(xb_bottom_z, "z", DOWN)

    xb_far = [
        lax.ppermute(after(xbt_below, xbb_below), "z", UP),
        lax.ppermute(xbb_above, "z", DOWN),
    ]
    yb_far = [lax.ppermute(yb_below[:quarter], "x", UP), lax.ppermute(yb_above[quarter:], "x", DOWN)]

    x_parts = [xm, xa_below, xa_above, *xa_far, xb_top, xb_bottom, xbt_below, xbb_below, xbt_above, xbb_above]
    y_parts = [ym, ya_below, ya_above, *ya_far, yb, yb_below, yb_above]
    own, far, x_late, y_late = early_product(x_parts, y_parts, where)
    far = late_product(1, where, xb_far, yb_far, x_late, y_late, far)
    peer = lax.ppermute(far, "c", SWAP)
    own = late_product(0, where, xb_far, yb_far, x_late, y_late, after(own, far))
    sign_next, payload = finish_and_payload(where, pattern_product.T, index, energy, xm, own, peer)
    received = exchange(payload)
    return sign_next, force_sums(received, force_h, force_s)


def solution(mesh):
    fine = Mesh(mesh.devices.reshape(2, 4, 2, 4, 2), AXES)
    row, col = ("yl", "x"), ("yh", "z", "c")
    in_specs = (
        P(row, col),
        P(row, col),
        P(row, col),
        P(row, col),
        P(row, col),
        P(row),
        P(AXES, None, None),
        P(AXES, None),
        P(AXES, None, None),
        P(AXES, None, None),
    )
    out_specs = (P(row, col), P(AXES))
    return jax.shard_map(shards, mesh=fine, in_specs=in_specs, out_specs=out_specs, check_vma=False)
```
